128 devices in a mesh: dp: 4 (over y), expert: 32 (over x, z, core).
Axes of the slice: x: 4, y: 4, z: 4, core: 2. Of those that a mesh axis runs over, the one named last changes fastest.
Arguments:
- hidden_in: bfloat16 [32768, 1024], P(('dp', 'expert')), may hold values from -6 to 6
- moe_gain: float32 [1024], replicated, may hold values from 0.1 to 1.9
- router_weight: bfloat16 [1024, 64], replicated, may hold values from -0.1875 to 0.1875
- expert_gate: bfloat16 [64, 1024, 1024], P('expert'), may hold values from -0.1875 to 0.1875
- expert_up: bfloat16 [64, 1024, 1024], P('expert'), may hold values from -0.1875 to 0.1875
- expert_down: bfloat16 [64, 1024, 1024], P('expert'), may hold values from -0.1875 to 0.1875
- final_gain: float32 [1024], replicated, may hold values from 0.1 to 1.9
- vocab_weight: bfloat16 [1024, 32768], P(None, 'expert'), may hold values from -24 to 24
- token_ids: int32 [32768], P(('dp', 'expert')), may hold values from 0 to 32767
- doc_ids: int32 [32768], P(('dp', 'expert')), may hold values from 0 to 511, as said below
- routes: int32 [32768, 2], P(('dp', 'expert')), may hold values from 0 to 63, all different within a row; in each aligned block of 256 rows (0 to 255, 256 to 511, ...) at most 16 rows name the same one
Outputs:
- token_loss: float32 [32768], P(('dp', 'expert'))
- doc_score: float32 [512], P(('dp', 'expert'))
The draws below stay inside these ranges and needn't reach their ends.
Inputs may be any that keep to these rules, and one draw needn't show every extreme that they name: `routes`: among the rows of one device no expert is named more than 16 times; in every draw some expert is named exactly 16 times by the rows of some device. `doc_ids`: documents are numbered in the order of the stream; each document is one run of consecutive tokens, shorter than 512; every document number is used; the rows of each device hold the first tokens of exactly 4 documents.
All inputs are finite; a program needn't handle non-finite values.
Results may differ from the reference program's by a relative error of at most 0.0031.
Values may be sent and summed in bfloat16 or wider, within the bound.
A program may use at most 128 MiB of HBM per device.

```python
import math
import jax
import jax.numpy as jnp
import numpy as np
from jax import lax

D = 1024
FF = 1024
V = 32768
TOP = 2
E = 64
TOK_DEV = 256
TOKENS = 32768
CAP = 16
DOC_DEV = 4
DOCS = 512
N_DP = 4
N_EXPERT = 32


def draw_vocab_weight(key, part):
    first_key = jax.random.fold_in(jax.random.fold_in(key, 7), 0)
    values = jnp.clip(jax.random.normal(first_key, (D, V), jnp.float32), -6.0, 6.0) * (3.0 / math.sqrt(D))
    return jnp.clip(values, -24.0, 24.0).astype(jnp.bfloat16)


def draw_doc_ids(key, part):
    holders = TOKENS // TOK_DEV
    device_keys = jax.random.split(jax.random.fold_in(key, 11), holders)

    def starts_of(one_key):
        order = jax.random.permutation(one_key, TOK_DEV - 1) + 1
        return order[:DOC_DEV].astype(jnp.int32)
    starts = jax.vmap(starts_of)(device_keys)
    starts = starts.at[0, 0].set(0)
    device_rows = jnp.arange(holders, dtype=jnp.int32)[:, None]
    flags = jnp.zeros((holders, TOK_DEV), jnp.int32).at[device_rows, starts].set(1)
    runs = jnp.cumsum(flags.reshape(-1)) - 1
    return runs.astype(jnp.int32)


def plant(array, key, low, largest):
    shape = array.shape
    spot = [jax.random.randint(jax.random.fold_in(key, axis), (), 0, shape[axis]) for axis in range(len(shape))]
    array = array.at[tuple(spot)].set(low)
    longest = shape.index(max(shape))
    spot[longest] = (spot[longest] + 1) % shape[longest]
    return array.at[tuple(spot)].set(largest)


def level_of(own_key, dims, cuts, least, largest):
    factor_of, own = 1.0, jax.random.fold_in(own_key, 6)
    for position, parts in cuts:
        steps = jnp.exp(jax.random.uniform(jax.random.fold_in(own, position), (parts,), jnp.float32, least / len(cuts), largest / len(cuts)))
        factor_of = factor_of * jnp.repeat(steps, dims[position] // parts).reshape([-1 if axis == position else 1 for axis in range(len(dims))])
    return factor_of


def cumulative_ranks(count, slope):
    weights = [(1 << 20) // math.isqrt(standing ** slope) + 1 for standing in range(1, count + 1)]
    deviation = 1 + sum(weights) // (1 << 30)
    return np.cumsum(np.array([max(1, weight // deviation) for weight in weights]))


def ranked(key, shape, amount, slope):
    listing = cumulative_ranks(amount, slope)
    pick = jax.random.randint(jax.random.fold_in(key, 1), shape, 0, int(listing[amount - 1]))
    standing = jnp.searchsorted(jnp.asarray(listing, jnp.int32), pick, side="right")
    return jax.random.permutation(jax.random.fold_in(key, 2), amount)[standing].astype(jnp.int32)


def assign_block(own_key, own, number, rows, number_of, top, reach, skew):
    sequence = jax.random.permutation(own_key, number_of)
    crowded, ordinary = shares(number_of, rows * top, reach, skew, True), shares(number_of, rows * top, reach, skew, False)
    places = jnp.arange(number_of)

    def named(tallies, offset_by):
        used = int((tallies > 0).sum())
        fixed = max(1, used // 4)
        moved = fixed + (places - fixed + offset_by * (used - fixed)) % max(1, number_of - fixed)
        return jnp.zeros((number_of,), jnp.int32).at[sequence[jnp.where(places < fixed, places, moved)]].set(jnp.asarray(tallies, jnp.int32))

    tallies = jnp.where(number % 4 == 0, named(crowded, number // 4), named(ordinary, number - number // 4 - 1))
    mixed = jax.random.permutation(jax.random.fold_in(own, 3), number_of)
    source_of, receiver = mixed[0:number_of // 2 * 2:2], mixed[1:number_of // 2 * 2:2]
    slack = jnp.minimum(tallies[source_of] - 1, reach - tallies[receiver]) // 2
    slack = jnp.where((source_of == sequence[0]) | (receiver == sequence[0]) | (tallies[receiver] == 0), 0, jnp.maximum(slack, 0))
    moved = jax.random.randint(jax.random.fold_in(own, 4), (number_of // 2,), 0, 1 << 20) % (slack + 1)
    tallies = tallies.at[source_of].add(-moved).at[receiver].add(moved)
    members = jnp.searchsorted(jnp.cumsum(tallies), jnp.arange(rows * top), side="right").astype(jnp.int32)
    table = members.reshape(top, rows).T
    table = table[jax.random.permutation(jax.random.fold_in(own, 1), rows)]
    offset_by = jax.random.randint(jax.random.fold_in(own, 2), (rows, 1), 0, top)
    return jnp.take_along_axis(table, (jnp.arange(top)[None, :] + offset_by) % top, axis=1)


def shares(count, total, limit, lean, full):
    weights = [(1 << 20) // math.isqrt(standing ** lean) + 1 for standing in range(1, count + 1)]
    largest = limit if full else min(limit, max(-(-total // count), total * weights[0] // sum(weights)))
    least = 1 if total - largest >= count - 1 else 0
    given, rest = [largest] + [least] * (count - 1), total - largest - least * (count - 1)
    while rest > 0:
        movable = [i for i in range(1, count) if given[i] < largest] or [i for i in range(1, count) if given[i] < limit]
        mass, budget = sum([weights[i] for i in movable]), rest
        for i in movable:
            extra = min(limit - given[i], max(1, budget * weights[i] // mass), rest)
            given[i] = given[i] + extra
            rest = rest - extra
    return np.array(given)


def centred(stream_key, extent, spread, reach, shards=(), kind=jnp.bfloat16):
    drawn = spread * jax.random.normal(stream_key, extent, jnp.float32)
    if shards:
        drawn = drawn * level_of(stream_key, extent, shards, -0.22, 0.18)
    return jnp.clip(drawn, -reach, reach).astype(kind)


def setup_inputs(seed: int = 0) -> dict:
    streams_of = jax.random.split(jax.random.key(seed), 12)
    hidden_in = centred(streams_of[0], (TOKENS, D), 1.0, 6.0, ((0, 128),))
    moe_gain = jnp.clip(1.0 + 0.18 * jax.random.normal(streams_of[1], (D,), jnp.float32), 0.1, 1.9)
    router_weight = centred(streams_of[2], (D, E), D ** -0.5, 0.1875)
    expert_gate = centred(streams_of[3], (E, D, FF), D ** -0.5, 0.1875, ((0, 32),))
    expert_up = centred(streams_of[4], (E, D, FF), D ** -0.5, 0.1875, ((0, 32),))
    expert_down = centred(streams_of[5], (E, FF, D), FF ** -0.5, 0.1875, ((0, 32),))
    final_gain = jnp.clip(1.0 + 0.18 * jax.random.normal(streams_of[6], (D,), jnp.float32), 0.1, 1.9)
    vocab_weight = draw_vocab_weight(jax.random.fold_in(streams_of[11], 71), 0)
    token_ids = plant(ranked(streams_of[8], (TOKENS,), V, 2), jax.random.fold_in(streams_of[8], 3), 0, V - 1).astype(jnp.int32)
    doc_ids = draw_doc_ids(jax.random.fold_in(streams_of[11], 71), 0)
    routes_keys = jax.random.split(jax.random.fold_in(streams_of[10], 1), TOKENS // TOK_DEV)
    routes_turns = jax.random.permutation(jax.random.fold_in(streams_of[10], 3), TOKENS // TOK_DEV)
    routes = jax.vmap(lambda own, number: assign_block(jax.random.fold_in(streams_of[10], 2), own, number, TOK_DEV, E, TOP, CAP, 2))(routes_keys, routes_turns).reshape((TOKENS, TOP))
    return dict(hidden_in=hidden_in, moe_gain=moe_gain, router_weight=router_weight, expert_gate=expert_gate, expert_up=expert_up, expert_down=expert_down, final_gain=final_gain, vocab_weight=vocab_weight, token_ids=token_ids, doc_ids=doc_ids, routes=routes)


EPSILON = 1e-06

def normalize(values, gain_vector):
    inv_scale = lax.rsqrt(lax.optimization_barrier(jnp.mean(values * values, axis=-1, keepdims=True)) + EPSILON)
    return values * inv_scale * gain_vector

def reference(hidden_in, moe_gain, router_weight, expert_gate, expert_up, expert_down, final_gain, vocab_weight, token_ids, doc_ids, routes):
    devices = N_DP * N_EXPERT
    residual = hidden_in.astype(jnp.float32)
    normed = normalize(residual, moe_gain).astype(jnp.bfloat16)
    router_scores = jnp.dot(normed, router_weight, preferred_element_type=jnp.float32)
    picked_scores = jnp.take_along_axis(router_scores, routes, axis=1)
    first_gate = jax.nn.sigmoid(picked_scores[:, 0] - picked_scores[:, 1])
    second_gate = 1.0 - first_gate
    flat_routes = routes.reshape(devices, TOK_DEV * TOP)
    one_hot = (flat_routes[:, :, None] == jnp.arange(E, dtype=jnp.int32)[None, None, :]).astype(jnp.int32)
    slot_index = lax.optimization_barrier(jnp.sum(one_hot * jnp.cumsum(one_hot, axis=1), axis=-1)) - 1
    source = jnp.arange(devices, dtype=jnp.int32)[:, None]
    target_slot = (flat_routes * (devices * CAP) + source * CAP + slot_index).reshape(-1).astype(jnp.int32)
    repeated = jnp.repeat(normed, TOP, axis=0)
    buffer = jnp.zeros((E * devices * CAP, D), jnp.bfloat16).at[target_slot].set(repeated)

    def run_expert(packed):
        inputs, weight_gate, weight_up, weight_down = packed
        gate_part = jnp.dot(inputs, weight_gate, preferred_element_type=jnp.float32)
        up_part = jnp.dot(inputs, weight_up, preferred_element_type=jnp.float32)
        active = (jax.nn.silu(gate_part) * up_part).astype(jnp.bfloat16)
        return jnp.dot(active, weight_down, preferred_element_type=jnp.float32).astype(jnp.bfloat16)
    results = lax.map(run_expert, (buffer.reshape(E, devices * CAP, D), expert_gate, expert_up, expert_down))
    outputs = results.reshape(E * devices * CAP, D)[target_slot].reshape(TOKENS, TOP, D).astype(jnp.float32)
    mixed = residual + (first_gate[:, None] * outputs[:, 0, :] + second_gate[:, None] * outputs[:, 1, :])
    final_rows = normalize(mixed, final_gain).astype(jnp.bfloat16)
    targets = jnp.concatenate([token_ids[1:], jnp.zeros((1,), jnp.int32)]).astype(jnp.int32)
    following = jnp.concatenate([doc_ids[1:], jnp.full((1,), -1, jnp.int32)])
    counted = following == doc_ids

    def head_block(packed):
        block_rows, block_targets = packed
        scores = jnp.dot(block_rows, vocab_weight, preferred_element_type=jnp.float32)
        highest = lax.optimization_barrier(jnp.max(scores, axis=1))
        log_norm = highest + jnp.log(lax.optimization_barrier(jnp.sum(jnp.exp(scores - highest[:, None]), axis=1)))
        target_score = jnp.take_along_axis(scores, block_targets[:, None], axis=1)[:, 0]
        return log_norm - target_score
    differences = lax.map(head_block, (final_rows.reshape(devices, TOK_DEV, D), targets.reshape(devices, TOK_DEV))).reshape(TOKENS)
    token_loss = jnp.where(counted, differences, jnp.zeros_like(differences))
    doc_loss = jax.ops.segment_sum(token_loss, doc_ids, num_segments=DOCS)
    doc_length = jax.ops.segment_sum(jnp.ones_like(token_loss), doc_ids, num_segments=DOCS)
    global_mean = jnp.sum(token_loss) / (TOKENS - DOCS)
    doc_score = doc_loss / doc_length - global_mean
    return (token_loss, doc_score)
```

```python
import jax
import jax.numpy as jnp
from jax import lax
from jax.experimental import pallas as pl
from jax.experimental.pallas import tpu as pltpu
from jax.sharding import PartitionSpec as P

TOP = 2
DOC_DEV = 4
SIDE = 4
OWNERS = 32
GROUPS = 4
BOTH = ("dp", "expert")
EPSILON = 1e-06
MESH_ID = pl.DeviceIdType.MESH


def normalize(values, gain_vector):
    inv_scale = lax.rsqrt(jnp.mean(values * values, axis=-1, keepdims=True) + EPSILON)
    return values * inv_scale * gain_vector


def place():
    own = lax.axis_index("expert")
    return own // 8, (own // 2) % SIDE, own % 2


def partner(i, sign):
    x, z, core = place()
    dx = (i % 8) // 2
    dz = (i // 8 + SIDE - dx) % SIDE
    dc = i % 2
    return ((x + sign * dx + SIDE) % SIDE) * 8 + ((z + sign * dz + SIDE) % SIDE) * 2 + (core + dc) % 2


def moe_kernel(
    hidden_ref, gain_ref, router_ref, routes_ref, final_gain_ref, gate_hbm, up_hbm, down_hbm,
    rows_ref,
    normed, outgoing, arrived, gate_w, up_w, down_w, result, returned, place_a, place_b, mixed,
    weight_sem, self_sem, send_out, recv_out, send_back, recv_back,
):
    tokens, width = hidden_ref.shape
    local = gate_hbm.shape[0]
    experts = OWNERS * local
    slots = outgoing.shape[2]
    part = local * slots
    per_group = OWNERS // GROUPS
    chunk = per_group * slots
    barrier = pltpu.get_barrier_semaphore()
    dp = lax.axis_index("dp")

    def to(device):
        return {"dp": dp, "expert": device}

    @pl.loop(1, OWNERS)
    def _(i):
        pl.semaphore_signal(barrier, inc=1, device_id=to(partner(i, 1)), device_id_type=MESH_ID)

    weights = []
    for n, (source, target) in enumerate(((gate_hbm, gate_w), (up_hbm, up_w), (down_hbm, down_w))):
        copy = pltpu.make_async_copy(source, target, weight_sem.at[n])
        copy.start()
        weights.append(copy)

    residual = hidden_ref[...].astype(jnp.float32)
    normed[...] = normalize(residual, gain_ref[...]).astype(jnp.bfloat16)
    router_scores = lax.dot_general(
        router_ref[...], normed[...], (((1,), (1,)), ((), ())), preferred_element_type=jnp.float32
    )
    first = routes_ref[0:1, :]
    second = routes_ref[1:2, :]
    expert_iota = lax.broadcasted_iota(jnp.int32, (experts, tokens), 0)
    is_first = expert_iota == first
    is_second = expert_iota == second
    member = jnp.where(is_first | is_second, 1.0, 0.0).astype(jnp.bfloat16)
    earlier = (
        lax.broadcasted_iota(jnp.int32, (tokens, tokens), 0) < lax.broadcasted_iota(jnp.int32, (tokens, tokens), 1)
    )
    rank = jnp.dot(
        member, jnp.where(earlier, 1.0, 0.0).astype(jnp.bfloat16), preferred_element_type=jnp.float32
    )
    x, z, core = place()

    def position(expert, chosen):
        owner = expert // local
        dx = (owner // 8 + SIDE - x) % SIDE
        dz = ((owner // 2) % SIDE + SIDE - z) % SIDE
        dc = (owner + core) % 2
        index = ((dx + dz) % SIDE) * 8 + dx * 2 + dc
        own_rank = jnp.sum(jnp.where(chosen, rank, 0.0), axis=0, keepdims=True).astype(jnp.int32)
        return index * part + (expert % local) * slots + own_rank

    first_pos = position(first, is_first)
    second_pos = position(second, is_second)

    for group in range(GROUPS):
        slot_iota = lax.broadcasted_iota(jnp.int32, (per_group * part, tokens), 0) + group * per_group * part
        chosen = (slot_iota == first_pos) | (slot_iota == second_pos)
        block = jnp.dot(
            jnp.where(chosen, 1.0, 0.0).astype(jnp.bfloat16), normed[...], preferred_element_type=jnp.float32
        )
        outgoing[pl.ds(group * per_group, per_group)] = block.astype(jnp.bfloat16).reshape(
            per_group, local, slots, width
        )
        if group == 0:
            own_copy = pltpu.make_async_copy(outgoing.at[0], arrived.at[:, pl.ds(0, slots)], self_sem)
            own_copy.start()
            pl.semaphore_wait(barrier, OWNERS - 1)

        @pl.loop(max(1, group * per_group), (group + 1) * per_group)
        def _(i):
            pltpu.make_async_remote_copy(
                src_ref=outgoing.at[i],
                dst_ref=arrived.at[:, pl.ds(pl.multiple_of(i * slots, slots), slots)],
                send_sem=send_out.at[i],
                recv_sem=recv_out.at[i],
                device_id=to(partner(i, 1)),
                device_id_type=MESH_ID,
            ).start()

    picked = jnp.sum(
        jnp.where(is_first, router_scores, 0.0) - jnp.where(is_second, router_scores, 0.0), axis=0, keepdims=True
    )
    first_gate = jax.nn.sigmoid(picked)
    lines = lax.broadcasted_iota(jnp.int32, (128, tokens), 0)
    table = jnp.where(
        lines == 0,
        first_pos.astype(jnp.float32),
        jnp.where(lines == 1, second_pos.astype(jnp.float32), jnp.where(lines == 2, first_gate, 0.0)),
    )
    columns = table.T
    lane_iota = lax.broadcasted_iota(jnp.int32, (tokens, experts * slots), 1).astype(jnp.float32)
    place_a[...] = jnp.where(lane_iota == columns[:, 0:1], 1.0, 0.0).astype(jnp.bfloat16)
    place_b[...] = jnp.where(lane_iota == columns[:, 1:2], 1.0, 0.0).astype(jnp.bfloat16)
    gate_a = columns[:, 2:3]
    gate_b = 1.0 - gate_a

    own_copy.wait()
    for copy in weights:
        copy.wait()

    def arrival(i):
        return pltpu.make_async_remote_copy(
            src_ref=outgoing.at[i],
            dst_ref=arrived.at[:, pl.ds(pl.multiple_of(i * slots, slots), slots)],
            send_sem=send_out.at[i],
            recv_sem=recv_out.at[i],
            device_id=to(partner(i, 1)),
            device_id_type=MESH_ID,
        )

    def back(i):
        return pltpu.make_async_remote_copy(
            src_ref=result.at[:, pl.ds(pl.multiple_of(i * slots, slots), slots)],
            dst_ref=returned.at[i],
            send_sem=send_back.at[i],
            recv_sem=recv_back.at[i],
            device_id=to(partner(i, -1)),
            device_id_type=MESH_ID,
        )

    for group in range(GROUPS):
        low, high = max(1, group * per_group), (group + 1) * per_group

        @pl.loop(low, high)
        def _(i):
            arrival(i).wait_recv()

        @pl.loop(0, local)
        def _(n):
            inputs = arrived[n, pl.ds(group * chunk, chunk)]
            gate_part = jnp.dot(inputs, gate_w[n], preferred_element_type=jnp.float32)
            up_part = jnp.dot(inputs, up_w[n], preferred_element_type=jnp.float32)
            active = (jax.nn.silu(gate_part) * up_part).astype(jnp.bfloat16)
            result[n, pl.ds(group * chunk, chunk)] = jnp.dot(
                active, down_w[n], preferred_element_type=jnp.float32
            ).astype(jnp.bfloat16)

        if group == 0:
            home = pltpu.make_async_copy(result.at[:, pl.ds(0, slots)], returned.at[0], self_sem)
            home.start()

        @pl.loop(low, high)
        def _(i):
            back(i).start()

    home.wait()
    mixed[...] = residual
    for group in range(GROUPS):
        low, high = max(1, group * per_group), (group + 1) * per_group

        @pl.loop(low, high)
        def _(i):
            back(i).wait_recv()

        block = returned[pl.ds(group * per_group, per_group)].reshape(per_group * part, width)
        span = slice(group * per_group * part, (group + 1) * per_group * part)
        mixed[...] += gate_a * jnp.dot(
            place_a[:, span], block, preferred_element_type=jnp.float32
        ) + gate_b * jnp.dot(place_b[:, span], block, preferred_element_type=jnp.float32)
    rows_ref[...] = normalize(mixed[...], final_gain_ref[...]).astype(jnp.bfloat16)

    @pl.loop(1, OWNERS)
    def _(i):
        arrival(i).wait_send()
        back(i).wait_send()


def moe(hidden_in, moe_gain, router_weight, expert_gate, expert_up, expert_down, final_gain, routes):
    tokens, width = hidden_in.shape
    local, _, hidden_units = expert_gate.shape
    experts = OWNERS * local
    slots = max(2, 2 * TOP * tokens // experts)
    bf16, f32 = jnp.bfloat16, jnp.float32
    vmem = pl.BlockSpec(memory_space=pltpu.VMEM)
    hbm = pl.BlockSpec(memory_space=pl.ANY)
    return pl.pallas_call(
        moe_kernel,
        out_shape=jax.ShapeDtypeStruct((tokens, width), bf16),
        in_specs=[vmem] * 5 + [hbm] * 3,
        out_specs=vmem,
        scratch_shapes=[
            pltpu.VMEM((tokens, width), bf16),
            pltpu.VMEM((OWNERS, local, slots, width), bf16),
            pltpu.VMEM((local, OWNERS * slots, width), bf16),
            pltpu.VMEM((local, width, hidden_units), bf16),
            pltpu.VMEM((local, width, hidden_units), bf16),
            pltpu.VMEM((local, hidden_units, width), bf16),
            pltpu.VMEM((local, OWNERS * slots, width), bf16),
            pltpu.VMEM((OWNERS, local, slots, width), bf16),
            pltpu.VMEM((tokens, experts * slots), bf16),
            pltpu.VMEM((tokens, experts * slots), bf16),
            pltpu.VMEM((tokens, width), f32),
            pltpu.SemaphoreType.DMA((3,)),
            pltpu.SemaphoreType.DMA,
            pltpu.SemaphoreType.DMA((OWNERS,)),
            pltpu.SemaphoreType.DMA((OWNERS,)),
            pltpu.SemaphoreType.DMA((OWNERS,)),
            pltpu.SemaphoreType.DMA((OWNERS,)),
        ],
        compiler_params=pltpu.CompilerParams(
            collective_id=0, has_side_effects=True, vmem_limit_bytes=48 * 2**20
        ),
        name="moe",
    )(
        hidden_in, moe_gain.reshape(1, width), router_weight.T, routes.T, final_gain.reshape(1, width),
        expert_gate, expert_up, expert_down,
    )


def stats_block(hidden_rows, wanted, vocab_weight, voc_start):
    scores = jnp.dot(hidden_rows, vocab_weight, preferred_element_type=jnp.float32)
    highest = jnp.max(scores, axis=1)
    totals = jnp.sum(jnp.exp(scores - highest[:, None]), axis=1)
    columns = voc_start + lax.broadcasted_iota(jnp.int32, scores.shape, 1)
    picked = jnp.sum(jnp.where(columns == wanted[:, None], scores, 0.0), axis=1)
    return jnp.stack([highest, totals, picked])


def local(
    hidden_in, moe_gain, router_weight, expert_gate, expert_up, expert_down, final_gain, vocab_weight,
    token_ids, doc_ids, routes,
):
    tok_rows, width = hidden_in.shape
    devices = lax.axis_size("dp") * OWNERS
    final_rows = moe(hidden_in, moe_gain, router_weight, expert_gate, expert_up, expert_down, final_gain, routes)
    heads = jnp.stack([token_ids[0], doc_ids[0]])
    following = lax.ppermute(heads, BOTH, [(k + 1, k) for k in range(devices - 1)])
    targets = jnp.concatenate([token_ids[1:], following[:1]])
    own = lax.axis_index("dp") * OWNERS + lax.axis_index("expert")
    doc_next = jnp.where(own == devices - 1, -1, following[1:])
    counted = jnp.concatenate([doc_ids[1:], doc_next]) == doc_ids
    voc_start = lax.axis_index("expert") * vocab_weight.shape[1]
    all_rows = lax.all_gather(final_rows, "expert", axis=0, tiled=True)
    all_targets = lax.all_gather(targets, "expert", axis=0, tiled=True)
    blocks = lax.map(
        lambda packed: stats_block(packed[0], packed[1], vocab_weight, voc_start),
        (all_rows.reshape(8, 1024, width), all_targets.reshape(8, 1024)),
    )
    stats = jnp.transpose(blocks, (0, 2, 1)).reshape(OWNERS, tok_rows, 3)
    stats = jnp.transpose(stats, (0, 2, 1))
    mine = lax.all_to_all(stats, "expert", split_axis=0, concat_axis=0, tiled=True)
    high = jnp.max(mine[:, 0], axis=0)
    totals = jnp.sum(mine[:, 1] * jnp.exp(mine[:, 0] - high), axis=0)
    token_loss = jnp.where(counted, high + jnp.log(totals) - jnp.sum(mine[:, 2], axis=0), 0.0)
    documents = DOC_DEV * devices
    member_map = (doc_ids[:, None] == lax.broadcasted_iota(jnp.int32, (tok_rows, documents), 1)).astype(jnp.float32)
    partial = jnp.stack(
        [jnp.dot(token_loss, member_map, precision=lax.Precision.HIGHEST), jnp.sum(member_map, axis=0)]
    )
    whole = lax.psum(partial, BOTH)
    pieces = lax.dynamic_slice_in_dim(whole, own * DOC_DEV, DOC_DEV, 1)
    global_mean = jnp.sum(whole[0]) / (tok_rows * devices - documents)
    return (token_loss, pieces[0] / pieces[1] - global_mean)


def solution(mesh):
    in_specs = (
        P(BOTH, None), P(), P(), P("expert", None, None), P("expert", None, None), P("expert", None, None), P(),
        P(None, "expert"), P(BOTH), P(BOTH), P(BOTH, None),
    )
    return jax.shard_map(local, mesh=mesh, in_specs=in_specs, out_specs=(P(BOTH), P(BOTH)), check_vma=False)
```

```python
import jax
import jax.numpy as jnp
from jax import lax
from jax.experimental import pallas as pl
from jax.experimental.pallas import tpu as pltpu
from jax.sharding import PartitionSpec as P

TOP = 2
DOC_DEV = 4
SIDE = 4
DP = 4
OWNERS = 32
GROUPS = 4
PEERS = 16
BOTH = ("dp", "expert")
EPSILON = 1e-06
MESH_ID = pl.DeviceIdType.MESH
STEP_SLOT = (0, 0, 4, 3, 1, 4, 3, 1, 2, 2, 5, 7, 6, 5, 7, 6)
STEP_HALF = (0, 1, 0, 0, 0, 1, 1, 1, 0, 1, 0, 0, 0, 1, 1, 1)


def normalize(values, gain_vector):
    inv_scale = lax.rsqrt(jnp.mean(values * values, axis=-1, keepdims=True) + EPSILON)
    return values * inv_scale * gain_vector


def looked_up(table, step):
    found = jnp.int32(table[0])
    for k in range(1, len(table)):
        found = jnp.where(step == k, jnp.int32(table[k]), found)
    return found


def kernel(
    hidden_hbm, gain_ref, router_ref, routes_ref, final_gain_ref, tokens_ref, docs_ref,
    gate_hbm, up_hbm, down_hbm, vocab_hbm,
    loss_ref, score_ref,
    hidden, normed, outgoing, arrived, gate_w, up_w, down_w, result, returned, place_a, place_b, mixed,
    own_raw, other_raw, vocab_t, rows, ids, next_ids, targets, stats_out, stats_in, sums_out, sums_in, lead_in,
    dp_out, dp_in,
    load_sem, self_sem, send_out, recv_out, send_back, recv_back, send_voc, recv_voc, send_ids, recv_ids,
    send_tgt, recv_tgt, send_rows, recv_rows, send_stats, recv_stats, send_sums, recv_sums, send_lead, recv_lead,
    send_dp, recv_dp,
):
    tokens, width = hidden.shape
    local = gate_hbm.shape[0]
    experts = OWNERS * local
    slots = outgoing.shape[2]
    part = local * slots
    per_group = OWNERS // GROUPS
    chunk = per_group * slots
    voc = vocab_hbm.shape[1]
    quarter = voc // DP
    half = tokens // 2
    dp = lax.axis_index("dp")
    own = lax.axis_index("expert")
    x, z, core = own // 8, (own // 2) % SIDE, own % 2
    linear = dp * OWNERS + own
    devices = DP * OWNERS
    mate_x = x + 1 - 2 * (x % 2)
    mirror = (SIDE - 1 - x) * 8 + z * 2 + core

    def at(device, plane=dp):
        return {"dp": plane, "expert": device}

    def shifted(steps):
        other = (linear + steps + devices) % devices
        return at(other % OWNERS, other // OWNERS)

    def partner(i, sign):
        dx = (i % 8) // 2
        dz = (i // 8 + SIDE - dx) % SIDE
        dc = i % 2
        return ((x + sign * dx + SIDE) % SIDE) * 8 + ((z + sign * dz + SIDE) % SIDE) * 2 + (core + dc) % 2

    def peer(q):
        jx, jz, jc = q // 8, (q // 2) % SIDE, q % 2
        return (x + jx * (mate_x - x)) * 8 + ((z + jz) % SIDE) * 2 + (core + jc) % 2

    def seen_from(q):
        return (q // 8) * 8 + ((SIDE - (q // 2) % SIDE) % SIDE) * 2 + q % 2

    def remote(source, target, send, recv, device):
        return pltpu.make_async_remote_copy(
            src_ref=source, dst_ref=target, send_sem=send, recv_sem=recv, device_id=device, device_id_type=MESH_ID
        )

    barrier = pltpu.get_barrier_semaphore()

    @pl.loop(1, OWNERS)
    def _(i):
        pl.semaphore_signal(barrier, inc=1, device_id=at(partner(i, 1)), device_id_type=MESH_ID)

    for dy in range(1, DP):
        pl.semaphore_signal(barrier, inc=1, device_id=at(own, (dp + dy) % DP), device_id_type=MESH_ID)
    for steps in (-1, 1):
        pl.semaphore_signal(barrier, inc=1, device_id=shifted(steps), device_id_type=MESH_ID)

    loads = []
    for n, (source, target) in enumerate(
        (
            (hidden_hbm, hidden),
            (gate_hbm, gate_w),
            (up_hbm, up_w),
            (down_hbm, down_w),
            (vocab_hbm, own_raw),
        )
    ):
        copy = pltpu.make_async_copy(source, target, load_sem.at[n])
        copy.start()
        loads.append(copy)

    ids[...] = jnp.zeros_like(ids)
    ids[0:2, :] = tokens_ref[...]
    ids[2:4, :] = docs_ref[...]
    pl.semaphore_wait(barrier, OWNERS - 1 + DP - 1 + 2)

    def columns(plane):
        return pl.ds(pl.multiple_of(plane * quarter, quarter), quarter)

    def voc_across():
        return remote(
            vocab_hbm.at[:, columns(dp)], other_raw.at[:, columns(dp)], send_voc.at[0], recv_voc.at[0], at(mirror)
        )

    def voc_along(dy, source):
        return remote(
            other_raw.at[:, columns(source)], other_raw.at[:, columns(source)], send_voc.at[dy], recv_voc.at[dy],
            at(own, (dp + dy) % DP),
        )

    def ids_copy():
        return remote(ids, next_ids, send_ids, recv_ids, shifted(-1))

    ids_copy().start()
    voc_across().start()

    loads[0].wait()
    normed[...] = normalize(hidden[...].astype(jnp.float32), gain_ref[...]).astype(jnp.bfloat16)
    first = routes_ref[0:1, :]
    second = routes_ref[1:2, :]
    expert_iota = lax.broadcasted_iota(jnp.int32, (experts, tokens), 0)
    is_first = expert_iota == first
    is_second = expert_iota == second
    member = jnp.where(is_first | is_second, 1.0, 0.0).astype(jnp.bfloat16)
    earlier = (
        lax.broadcasted_iota(jnp.int32, (tokens, tokens), 0) < lax.broadcasted_iota(jnp.int32, (tokens, tokens), 1)
    )
    rank = jnp.dot(
        member, jnp.where(earlier, 1.0, 0.0).astype(jnp.bfloat16), preferred_element_type=jnp.float32
    )

    def position(expert, chosen):
        owner = expert // local
        dx = (owner // 8 + SIDE - x) % SIDE
        dz = ((owner // 2) % SIDE + SIDE - z) % SIDE
        dc = (owner + core) % 2
        index = ((dx + dz) % SIDE) * 8 + dx * 2 + dc
        own_rank = jnp.sum(jnp.where(chosen, rank, 0.0), axis=0, keepdims=True).astype(jnp.int32)
        return index * part + (expert % local) * slots + own_rank

    first_pos = position(first, is_first)
    second_pos = position(second, is_second)

    def slot_rows(i):
        return pl.ds(pl.multiple_of(i * slots, slots), slots)

    def out(i):
        return remote(
            outgoing.at[i], arrived.at[:, slot_rows(i)], send_out.at[i], recv_out.at[i], at(partner(i, 1))
        )

    def back(i):
        return remote(
            result.at[:, slot_rows(i)], returned.at[i], send_back.at[i], recv_back.at[i], at(partner(i, -1))
        )

    for group in range(GROUPS):
        slot_iota = lax.broadcasted_iota(jnp.int32, (per_group * part, tokens), 0) + group * per_group * part
        chosen = (slot_iota == first_pos) | (slot_iota == second_pos)
        block = jnp.dot(
            jnp.where(chosen, 1.0, 0.0).astype(jnp.bfloat16), normed[...], preferred_element_type=jnp.float32
        )
        outgoing[pl.ds(group * per_group, per_group)] = block.astype(jnp.bfloat16).reshape(
            per_group, local, slots, width
        )
        if group == 0:
            own_copy = pltpu.make_async_copy(outgoing.at[0], arrived.at[:, pl.ds(0, slots)], self_sem)
            own_copy.start()

        @pl.loop(max(1, group * per_group), (group + 1) * per_group)
        def _(i):
            out(i).start()

    ids_copy().wait_recv()
    row_iota = lax.broadcasted_iota(jnp.int32, ids.shape, 0)
    lane_iota = lax.broadcasted_iota(jnp.int32, ids.shape, 1)
    own_ids = ids[...]
    after = pltpu.roll(own_ids, half - 1, 1)
    ends = lane_iota == half - 1
    after = jnp.where(ends & (row_iota == 0), own_ids[1:2, 0:1], after)
    after = jnp.where(ends & (row_iota == 1), next_ids[0:1, 0:1], after)
    after = jnp.where(ends & (row_iota == 2), own_ids[3:4, 0:1], after)
    after = jnp.where(ends & (row_iota == 3), next_ids[2:3, 0:1], after)
    targets[0] = after

    def target_copy(q):
        there = seen_from(q)
        return remote(targets.at[0], targets.at[there], send_tgt.at[q], recv_tgt.at[there], at(peer(q)))

    @pl.loop(1, PEERS)
    def _(q):
        target_copy(q).start()

    router_scores = lax.dot_general(
        router_ref[...], normed[...], (((1,), (1,)), ((), ())), preferred_element_type=jnp.float32
    )
    picked = jnp.sum(
        jnp.where(is_first, router_scores, 0.0) - jnp.where(is_second, router_scores, 0.0), axis=0, keepdims=True
    )
    first_gate = jax.nn.sigmoid(picked)
    lines = lax.broadcasted_iota(jnp.int32, (128, tokens), 0)
    table = jnp.where(
        lines == 0,
        first_pos.astype(jnp.float32),
        jnp.where(lines == 1, second_pos.astype(jnp.float32), jnp.where(lines == 2, first_gate, 0.0)),
    )
    per_token = table.T
    place_iota = lax.broadcasted_iota(jnp.int32, (tokens, experts * slots), 1).astype(jnp.float32)
    place_a[...] = jnp.where(place_iota == per_token[:, 0:1], 1.0, 0.0).astype(jnp.bfloat16)
    place_b[...] = jnp.where(place_iota == per_token[:, 1:2], 1.0, 0.0).astype(jnp.bfloat16)
    gate_a = per_token[:, 2:3]
    gate_b = 1.0 - gate_a

    loads[4].wait()

    @pl.loop(0, voc // 128)
    def _(j):
        strip = pl.ds(pl.multiple_of(j * 128, 128), 128)
        vocab_t[strip, :] = own_raw[:, strip].T

    voc_across().wait_recv()
    for dy in range(1, DP):
        voc_along(dy, dp).start()

    own_copy.wait()
    for copy in loads[1:4]:
        copy.wait()

    for group in range(GROUPS):
        low, high = max(1, group * per_group), (group + 1) * per_group

        @pl.loop(low, high)
        def _(i):
            out(i).wait_recv()

        @pl.loop(0, local)
        def _(n):
            inputs = arrived[n, pl.ds(group * chunk, chunk)]
            gate_part = jnp.dot(inputs, gate_w[n], preferred_element_type=jnp.float32)
            up_part = jnp.dot(inputs, up_w[n], preferred_element_type=jnp.float32)
            active = (jax.nn.silu(gate_part) * up_part).astype(jnp.bfloat16)
            result[n, pl.ds(group * chunk, chunk)] = jnp.dot(
                active, down_w[n], preferred_element_type=jnp.float32
            ).astype(jnp.bfloat16)

        if group == 0:
            home = pltpu.make_async_copy(result.at[:, pl.ds(0, slots)], returned.at[0], self_sem)
            home.start()

        @pl.loop(low, high)
        def _(i):
            back(i).start()

    for dy in range(DP):
        source = (dp + DP - dy) % DP
        if dy:
            voc_along(dy, source).wait_recv()

        @pl.loop(0, quarter // 128)
        def _(j):
            start = source * quarter + j * 128
            vocab_t[pl.ds(pl.multiple_of(voc + start, 128), 128), :] = other_raw[
                :, pl.ds(pl.multiple_of(start, 128), 128)
            ].T

    home.wait()
    mixed[...] = hidden[...].astype(jnp.float32)
    for group in range(GROUPS):
        low, high = max(1, group * per_group), (group + 1) * per_group

        @pl.loop(low, high)
        def _(i):
            back(i).wait_recv()

        block = returned[pl.ds(group * per_group, per_group)].reshape(per_group * part, width)
        span = slice(group * per_group * part, (group + 1) * per_group * part)
        mixed[...] += gate_a * jnp.dot(
            place_a[:, span], block, preferred_element_type=jnp.float32
        ) + gate_b * jnp.dot(place_b[:, span], block, preferred_element_type=jnp.float32)
    final_rows = normalize(mixed[...], final_gain_ref[...]).astype(jnp.bfloat16)
    rows[0, 0, 0] = final_rows[:half]
    rows[0, 1, 0] = final_rows[half:]

    above = x * 8 + ((z + 1) % SIDE) * 2 + core
    below = x * 8 + ((z + SIDE - 1) % SIDE) * 2 + core
    mate = mate_x * 8 + z * 2 + core
    sibling = x * 8 + z * 2 + 1 - core
    sends = []

    def row_copy(slot, h, there, device, side=0):
        number = len(sends)

        def made():
            return remote(
                rows.at[slot, h, 0], rows.at[there, h, side], send_rows.at[number],
                recv_rows.at[(there * 2 + h) * 2 + side], at(device),
            )

        sends.append(made)
        return made

    def row_arrival(slot, h, side):
        return remote(
            rows.at[slot, h, side], rows.at[slot, h, side], send_rows.at[0],
            recv_rows.at[(slot * 2 + h) * 2 + side], at(sibling),
        )

    onward = {}
    for h in range(2):
        onward[0, h] = [
            row_copy(0, h, 3, above), row_copy(0, h, 1, below), row_copy(0, h, 4, mate), row_copy(0, h, 0, sibling, 1)
        ]
        onward[4, h] = [row_copy(4, h, 7, above), row_copy(4, h, 5, below)]
        onward[3, h] = [row_copy(3, 0, 2, above)] if h == 0 else []
        onward[1, h] = [row_copy(1, 1, 2, below)] if h == 1 else []
        onward[2, h] = [row_copy(2, h, 6, mate)]
        for slot in range(1, 8):
            onward.setdefault((slot, h), []).append(row_copy(slot, h, slot, sibling, 1))
    for h in range(2):
        for made in onward[0, h]:
            made().start()

    @pl.loop(1, PEERS)
    def _(q):
        target_copy(seen_from(q)).wait_recv()

    own_base = own * voc
    other_base = mirror * voc
    tile = voc // 2

    def stats_copy(q):
        there = seen_from(q)
        return remote(stats_out.at[q], stats_in.at[there], send_stats.at[q], recv_stats.at[there], at(peer(q)))

    @pl.loop(0, PEERS)
    def _(q):
        stats_out[q] = jnp.zeros(stats_out.shape[1:], jnp.float32)

    @pl.loop(0, len(STEP_SLOT))
    def _(step):
        slot = looked_up(STEP_SLOT, step)
        h = looked_up(STEP_HALF, step)
        for k in range(2, len(STEP_SLOT)):

            @pl.when(step == k)
            def _():
                row_arrival(STEP_SLOT[k], STEP_HALF[k], 0).wait_recv()
                for made in onward[STEP_SLOT[k], STEP_HALF[k]]:
                    made().start()

        row_arrival(slot, h, 1).wait_recv()
        block = rows[slot, h].reshape(2 * half, width)
        wanted = jnp.concatenate(
            [targets[2 * slot, pl.ds(h, 1), :], targets[2 * slot + 1, pl.ds(h, 1), :]], axis=1
        )
        high = total = hit = None
        for n in range(4):
            scores = lax.dot_general(
                vocab_t[n * tile : (n + 1) * tile, :], block, (((1,), (1,)), ((), ())),
                preferred_element_type=jnp.float32,
            )
            base = (own_base if n < 2 else other_base) + (n % 2) * tile
            match = lax.broadcasted_iota(jnp.int32, scores.shape, 0) == wanted - base
            stacked = scores.reshape(tile // 8, 8, 2 * half)
            found = jnp.sum(jnp.where(match, scores, 0.0).reshape(stacked.shape), axis=0)
            top = jnp.max(stacked, axis=0)
            if n:
                top = jnp.maximum(top, high)
            summed = jnp.sum(jnp.exp(stacked - top[None]), axis=0)
            if n:
                summed = summed + total * jnp.exp(high - top)
                found = found + hit
            high, total, hit = top, summed, found
        top = jnp.max(high, axis=0, keepdims=True)
        summed = jnp.sum(total * jnp.exp(high - top), axis=0, keepdims=True)
        found = jnp.sum(hit, axis=0, keepdims=True)
        for side in range(2):
            lanes = slice(side * half, (side + 1) * half)
            stats_out[2 * slot + side, pl.ds(h, 1), :] = top[:, lanes]
            stats_out[2 * slot + side, pl.ds(2 + h, 1), :] = summed[:, lanes]
            stats_out[2 * slot + side, pl.ds(4 + h, 1), :] = found[:, lanes]

        @pl.when(h == 1)
        def _():
            @pl.when(slot > 0)
            def _():
                stats_copy(2 * slot).start()

            stats_copy(2 * slot + 1).start()

    stats_in[0] = stats_out[0]

    @pl.loop(1, PEERS)
    def _(q):
        stats_copy(seen_from(q)).wait_recv()

    every = stats_in[...]
    top = jnp.max(every[:, 0:2], axis=0)
    summed = jnp.sum(every[:, 2:4] * jnp.exp(every[:, 0:2] - top[None]), axis=0)
    found = jnp.sum(every[:, 4:6], axis=0)
    docs = docs_ref[...]
    two_rows = lax.broadcasted_iota(jnp.int32, docs.shape, 0)
    two_lanes = lax.broadcasted_iota(jnp.int32, docs.shape, 1)
    at_end = (two_rows == 1) & (two_lanes == half - 1) & (linear == devices - 1)
    counted = (targets[0, 2:4, :] == docs) & jnp.logical_not(at_end)
    token_loss = jnp.where(counted, top + jnp.log(summed) - found, 0.0)
    loss_ref[...] = token_loss

    def whole(values):
        return jnp.sum(jnp.sum(values, axis=1, keepdims=True), axis=0, keepdims=True)

    def of_document(number):
        mask = docs == number
        return whole(jnp.where(mask, token_loss, 0.0)), whole(jnp.where(mask, 1.0, 0.0))

    lead_loss, lead_length = of_document(DOC_DEV * linear - 1)
    lines = lax.broadcasted_iota(jnp.int32, (8, 128), 0)
    sums_out[...] = jnp.where(
        lines == 0, whole(token_loss), jnp.where(lines == 1, lead_loss, jnp.where(lines == 2, lead_length, 0.0))
    )

    def sum_copy(i):
        return remote(sums_out, sums_in.at[i], send_sums.at[i], recv_sums.at[i], at(partner(i, 1)))

    def lead_copy():
        return remote(sums_out, lead_in, send_lead, recv_lead, shifted(-1))

    @pl.loop(1, OWNERS)
    def _(i):
        sum_copy(i).start()

    lead_copy().start()
    sums_in[0] = sums_out[...]
    parts = [of_document(DOC_DEV * linear + j) for j in range(DOC_DEV)]

    @pl.loop(1, OWNERS)
    def _(i):
        sum_copy(i).wait_recv()

    dp_out[...] = jnp.sum(sums_in[...], axis=0)

    def dp_copy(dy):
        return remote(dp_out, dp_in.at[dy], send_dp.at[dy], recv_dp.at[dy], at(own, (dp + dy) % DP))

    for dy in range(1, DP):
        dp_copy(dy).start()
    lead_copy().wait_recv()
    dp_in[0] = dp_out[...]
    for dy in range(1, DP):
        dp_copy(dy).wait_recv()
    global_sum = jnp.sum(dp_in[...], axis=0)[0:1, 0:1]
    global_mean = global_sum / (tokens * devices - DOC_DEV * devices)
    lanes = lax.broadcasted_iota(jnp.int32, (1, 128), 1)
    scores = jnp.zeros((1, 128), jnp.float32)
    for j, (part_loss, part_length) in enumerate(parts):
        if j == DOC_DEV - 1:
            part_loss = part_loss + lead_in[1:2, 0:1]
            part_length = part_length + lead_in[2:3, 0:1]
        scores = jnp.where(lanes == j, part_loss / part_length - global_mean, scores)
    score_ref[...] = scores[:, 0:DOC_DEV]

    @pl.loop(1, OWNERS)
    def _(i):
        out(i).wait_send()
        back(i).wait_send()
        sum_copy(i).wait_send()

    @pl.loop(1, PEERS)
    def _(q):
        target_copy(q).wait_send()
        stats_copy(q).wait_send()

    voc_across().wait_send()
    ids_copy().wait_send()
    lead_copy().wait_send()
    for dy in range(1, DP):
        voc_along(dy, dp).wait_send()
        dp_copy(dy).wait_send()
    for made in sends:
        made().wait_send()


def local(
    hidden_in, moe_gain, router_weight, expert_gate, expert_up, expert_down, final_gain, vocab_weight,
    token_ids, doc_ids, routes,
):
    tokens, width = hidden_in.shape
    here, _, hidden_units = expert_gate.shape
    voc = vocab_weight.shape[1]
    experts = OWNERS * here
    slots = max(2, 2 * TOP * tokens // experts)
    half = tokens // 2
    bf16, f32, i32 = jnp.bfloat16, jnp.float32, jnp.int32
    vmem = pl.BlockSpec(memory_space=pltpu.VMEM)
    hbm = pl.BlockSpec(memory_space=pl.ANY)
    dma = pltpu.SemaphoreType.DMA
    loss, score = pl.pallas_call(
        kernel,
        out_shape=(jax.ShapeDtypeStruct((2, half), f32), jax.ShapeDtypeStruct((1, DOC_DEV), f32)),
        in_specs=[hbm] + [vmem] * 6 + [hbm] * 4,
        out_specs=(vmem, vmem),
        scratch_shapes=[
            pltpu.VMEM((tokens, width), bf16),
            pltpu.VMEM((tokens, width), bf16),
            pltpu.VMEM((OWNERS, here, slots, width), bf16),
            pltpu.VMEM((here, OWNERS * slots, width), bf16),
            pltpu.VMEM((here, width, hidden_units), bf16),
            pltpu.VMEM((here, width, hidden_units), bf16),
            pltpu.VMEM((here, hidden_units, width), bf16),
            pltpu.VMEM((here, OWNERS * slots, width), bf16),
            pltpu.VMEM((OWNERS, here, slots, width), bf16),
            pltpu.VMEM((tokens, experts * slots), bf16),
            pltpu.VMEM((tokens, experts * slots), bf16),
            pltpu.VMEM((tokens, width), f32),
            pltpu.VMEM((width, voc), bf16),
            pltpu.VMEM((width, voc), bf16),
            pltpu.VMEM((2 * voc, width), bf16),
            pltpu.VMEM((8, 2, 2, half, width), bf16),
            pltpu.VMEM((8, half), i32),
            pltpu.VMEM((8, half), i32),
            pltpu.VMEM((PEERS, 8, half), i32),
            pltpu.VMEM((PEERS, 8, half), f32),
            pltpu.VMEM((PEERS, 8, half), f32),
            pltpu.VMEM((8, 128), f32),
            pltpu.VMEM((OWNERS, 8, 128), f32),
            pltpu.VMEM((8, 128), f32),
            pltpu.VMEM((8, 128), f32),
            pltpu.VMEM((DP, 8, 128), f32),
            dma((5,)),
            dma,
            dma((OWNERS,)),
            dma((OWNERS,)),
            dma((OWNERS,)),
            dma((OWNERS,)),
            dma((DP,)),
            dma((DP,)),
            dma,
            dma,
            dma((PEERS,)),
            dma((PEERS,)),
            dma((32,)),
            dma((32,)),
            dma((PEERS,)),
            dma((PEERS,)),
            dma((OWNERS,)),
            dma((OWNERS,)),
            dma,
            dma,
            dma((DP,)),
            dma((DP,)),
        ],
        compiler_params=pltpu.CompilerParams(
            collective_id=0, has_side_effects=True, vmem_limit_bytes=58 * 2**20
        ),
        name="scoring",
    )(
        hidden_in, moe_gain.reshape(1, width), router_weight.T, routes.T, final_gain.reshape(1, width),
        token_ids.reshape(2, half), doc_ids.reshape(2, half), expert_gate, expert_up, expert_down, vocab_weight,
    )
    return loss.reshape(tokens), score.reshape(DOC_DEV)


def solution(mesh):
    in_specs = (
        P(BOTH, None), P(), P(), P("expert", None, None), P("expert", None, None), P("expert", None, None), P(),
        P(None, "expert"), P(BOTH), P(BOTH), P(BOTH, None),
    )
    return jax.shard_map(local, mesh=mesh, in_specs=in_specs, out_specs=(P(BOTH), P(BOTH)), check_vma=False)
```

```python
import jax
import jax.numpy as jnp
from jax import lax
from jax.experimental import pallas as pl
from jax.experimental.pallas import tpu as pltpu
from jax.sharding import PartitionSpec as P
TOP = 2
DOC_DEV = 4
SIDE = 4
DP = 4
OWNERS = 32
GROUPS = 4
PEERS = 16
BOTH = ('dp', 'expert')
ABOVE, BELOW, MATE, SIBLING = ("above", "below", "mate", "sibling")
FIRST_SENDS = (
    (0, 0, ABOVE), (0, 0, BELOW), (0, 0, MATE), (0, 0, SIBLING), (0, 1, ABOVE), (0, 1, BELOW), (0, 1, MATE), (0, 1, SIBLING),
)
SCHEDULE = (
    ((0, 0), (1, 0), (4, 0), (1, 0, BELOW), (4, 0, SIBLING), (1, 0, MATE), (4, 0, ABOVE),),
    ((4, 0),),
    ((0, 1),),
    ((4, 1), (1, 1), (4, 1), (1, 1, SIBLING), (3, 1), (1, 1, BELOW), (3, 0), (4, 1, SIBLING), (3, 1, MATE), (4, 1, BELOW), (3, 1, SIBLING),),
    ((1, 1),),
    ((3, 1), (5, 0), (3, 0, SIBLING), (7, 0), (7, 0, ABOVE), (1, 0, SIBLING), (7, 0, SIBLING), (5, 0, SIBLING),),
    ((7, 0),),
    ((3, 0), (2, 0), (2, 0, SIBLING),),
    ((2, 0), (2, 1), (2, 1, MATE), (7, 1), (2, 1, SIBLING),),
    ((1, 0),),
    ((5, 0), (6, 0),),
    ((2, 1), (6, 0, SIBLING),),
    ((6, 0), (7, 1, SIBLING), (5, 1),),
    ((7, 1), (6, 1), (5, 1, SIBLING), (6, 1, SIBLING),),
    ((6, 1),),
    ((5, 1),),
)
EPSILON = 1e-06
MESH_ID = pl.DeviceIdType.MESH
EPSILON = 1e-06

def normalize(values, gain_vector):
    inv_scale = lax.rsqrt(jnp.mean(values * values, axis=-1, keepdims=True) + EPSILON)
    return values * inv_scale * gain_vector

def looked_up(table, step):
    found = jnp.int32(table[0])
    for k in range(1, len(table)):
        found = jnp.where(step == k, jnp.int32(table[k]), found)
    return found

def kernel(hidden_hbm, gain_ref, router_ref, routes_ref, final_gain_ref, tokens_ref, docs_ref, gate_hbm, up_hbm, down_hbm, vocab_hbm, made_ref, hidden, normed, outgoing, arrived, gate_w, up_w, down_w, result, returned, place_a, place_b, mixed, own_raw, other_raw, vocab_t, rows, ids, next_ids, targets, stats_out, stats_in, sums_out, sums_in, lead_in, wide_out, wide_in, load_sem, self_sem, send_out, recv_out, send_back, recv_back, send_voc, recv_voc, send_ids, recv_ids, send_tgt, recv_tgt, send_rows, recv_rows, send_stats, recv_stats, send_sums, recv_sums, send_lead, recv_lead, send_wide, recv_wide):
    tokens, width = hidden.shape
    local = gate_hbm.shape[0]
    experts = OWNERS * local
    slots = outgoing.shape[2]
    part = local * slots
    per_group = OWNERS // GROUPS
    chunk = per_group * slots
    voc = vocab_hbm.shape[1]
    quarter = voc // DP
    half = tokens // 2
    dp = lax.axis_index('dp')
    own = lax.axis_index('expert')
    x, z, core = (own // 8, own // 2 % SIDE, own % 2)
    linear = dp * OWNERS + own
    devices = DP * OWNERS
    mate_x = x + 1 - 2 * (x % 2)
    mirror = (SIDE - 1 - x) * 8 + z * 2 + core

    def at(device, plane=dp):
        return {'dp': plane, 'expert': device}

    def shifted(steps):
        other = (linear + steps + devices) % devices
        return at(other % OWNERS, other // OWNERS)

    def partner(i, sign):
        dx = i % 8 // 2
        dz = (i // 8 + SIDE - dx) % SIDE
        dc = i % 2
        return (x + sign * dx + SIDE) % SIDE * 8 + (z + sign * dz + SIDE) % SIDE * 2 + (core + dc) % 2

    def peer(q):
        jx, jz, jc = (q // 8, q // 2 % SIDE, q % 2)
        return (x + jx * (mate_x - x)) * 8 + (z + jz) % SIDE * 2 + (core + jc) % 2

    def seen_from(q):
        return q // 8 * 8 + (SIDE - q // 2 % SIDE) % SIDE * 2 + q % 2

    def across(i):
        return (own if i % 2 == 0 else mirror, (dp + i // 2) % DP)

    def remote(source, target, send, recv, device):
        return pltpu.make_async_remote_copy(src_ref=source, dst_ref=target, send_sem=send, recv_sem=recv, device_id=device, device_id_type=MESH_ID)
    barrier = pltpu.get_barrier_semaphore()

    @pl.loop(1, OWNERS)
    def _(i):
        pl.semaphore_signal(barrier, inc=1, device_id=at(partner(i, 1)), device_id_type=MESH_ID)
    for i in range(2, 2 * DP):
        device, plane = across(i)
        pl.semaphore_signal(barrier, inc=1, device_id=at(device, plane), device_id_type=MESH_ID)
    for steps in (-1, 1):
        pl.semaphore_signal(barrier, inc=1, device_id=shifted(steps), device_id_type=MESH_ID)
    loads = []
    for n, (source, target) in enumerate(((hidden_hbm, hidden), (gate_hbm, gate_w), (up_hbm, up_w), (down_hbm, down_w), (vocab_hbm, own_raw))):
        copy = pltpu.make_async_copy(source, target, load_sem.at[n])
        copy.start()
        loads.append(copy)
    ids[...] = jnp.zeros_like(ids)
    ids[0:2, :] = tokens_ref[...]
    ids[2:4, :] = docs_ref[...]
    pl.semaphore_wait(barrier, OWNERS - 1 + 2 * (DP - 1) + 2)

    def columns(plane):
        return pl.ds(pl.multiple_of(plane * quarter, quarter), quarter)

    def voc_across(piece):
        span = pl.ds(pl.multiple_of(dp * quarter + piece * (quarter // 2), quarter // 2), quarter // 2)
        n = piece * DP
        return remote(vocab_hbm.at[:, span], other_raw.at[:, span], send_voc.at[n], recv_voc.at[n], at(mirror))

    def voc_along(dy, source):
        return remote(other_raw.at[:, columns(source)], other_raw.at[:, columns(source)], send_voc.at[dy], recv_voc.at[dy], at(own, (dp + dy) % DP))

    def ids_copy():
        return remote(ids, next_ids, send_ids, recv_ids, shifted(-1))
    ids_copy().start()
    for piece in range(2):
        voc_across(piece).start()
    loads[0].wait()
    normed[...] = normalize(hidden[...].astype(jnp.float32), gain_ref[...]).astype(jnp.bfloat16)
    first = routes_ref[0:1, :]
    second = routes_ref[1:2, :]
    expert_iota = lax.broadcasted_iota(jnp.int32, (experts, tokens), 0)
    is_first = expert_iota == first
    is_second = expert_iota == second
    member = jnp.where(is_first | is_second, 1.0, 0.0).astype(jnp.bfloat16)
    earlier = lax.broadcasted_iota(jnp.int32, (tokens, tokens), 0) < lax.broadcasted_iota(jnp.int32, (tokens, tokens), 1)
    rank = jnp.dot(member, jnp.where(earlier, 1.0, 0.0).astype(jnp.bfloat16), preferred_element_type=jnp.float32)

    def position(expert, chosen):
        owner = expert // local
        dx = (owner // 8 + SIDE - x) % SIDE
        dz = (owner // 2 % SIDE + SIDE - z) % SIDE
        dc = (owner + core) % 2
        index = (dx + dz) % SIDE * 8 + dx * 2 + dc
        own_rank = jnp.sum(jnp.where(chosen, rank, 0.0), axis=0, keepdims=True).astype(jnp.int32)
        return index * part + expert % local * slots + own_rank
    first_pos = position(first, is_first)
    second_pos = position(second, is_second)

    def slot_rows(i):
        return pl.ds(pl.multiple_of(i * slots, slots), slots)

    def out(i):
        return remote(outgoing.at[i], arrived.at[:, slot_rows(i)], send_out.at[i], recv_out.at[i], at(partner(i, 1)))

    def back(i):
        return remote(result.at[:, slot_rows(i)], returned.at[i], send_back.at[i], recv_back.at[i], at(partner(i, -1)))
    for group in range(GROUPS):
        slot_iota = lax.broadcasted_iota(jnp.int32, (per_group * part, tokens), 0) + group * per_group * part
        chosen = (slot_iota == first_pos) | (slot_iota == second_pos)
        block = jnp.dot(jnp.where(chosen, 1.0, 0.0).astype(jnp.bfloat16), normed[...], preferred_element_type=jnp.float32)
        outgoing[pl.ds(group * per_group, per_group)] = block.astype(jnp.bfloat16).reshape(per_group, local, slots, width)
        if group == 0:
            own_copy = pltpu.make_async_copy(outgoing.at[0], arrived.at[:, pl.ds(0, slots)], self_sem)
            own_copy.start()

        @pl.loop(max(1, group * per_group), (group + 1) * per_group)
        def _(i):
            out(i).start()
    ids_copy().wait_recv()
    row_iota = lax.broadcasted_iota(jnp.int32, ids.shape, 0)
    lane_iota = lax.broadcasted_iota(jnp.int32, ids.shape, 1)
    own_ids = ids[...]
    after = pltpu.roll(own_ids, half - 1, 1)
    ends = lane_iota == half - 1
    after = jnp.where(ends & (row_iota == 0), own_ids[1:2, 0:1], after)
    after = jnp.where(ends & (row_iota == 1), next_ids[0:1, 0:1], after)
    after = jnp.where(ends & (row_iota == 2), own_ids[3:4, 0:1], after)
    after = jnp.where(ends & (row_iota == 3), next_ids[2:3, 0:1], after)
    targets[0] = after

    def target_copy(q):
        there = seen_from(q)
        return remote(targets.at[0], targets.at[there], send_tgt.at[q], recv_tgt.at[there], at(peer(q)))

    @pl.loop(1, PEERS)
    def _(q):
        target_copy(q).start()
    router_scores = lax.dot_general(router_ref[...], normed[...], (((1,), (1,)), ((), ())), preferred_element_type=jnp.float32)
    picked = jnp.sum(jnp.where(is_first, router_scores, 0.0) - jnp.where(is_second, router_scores, 0.0), axis=0, keepdims=True)
    first_gate = jax.nn.sigmoid(picked)
    lines = lax.broadcasted_iota(jnp.int32, (128, tokens), 0)
    table = jnp.where(lines == 0, first_pos.astype(jnp.float32), jnp.where(lines == 1, second_pos.astype(jnp.float32), jnp.where(lines == 2, first_gate, 0.0)))
    per_token = table.T
    place_iota = lax.broadcasted_iota(jnp.int32, (tokens, experts * slots), 1).astype(jnp.float32)
    place_a[...] = jnp.where(place_iota == per_token[:, 0:1], 1.0, 0.0).astype(jnp.bfloat16)
    place_b[...] = jnp.where(place_iota == per_token[:, 1:2], 1.0, 0.0).astype(jnp.bfloat16)
    gate_a = per_token[:, 2:3]
    gate_b = 1.0 - gate_a
    loads[4].wait()

    @pl.loop(0, voc // 128)
    def _(j):
        strip = pl.ds(pl.multiple_of(j * 128, 128), 128)
        vocab_t[strip, :] = own_raw[:, strip].T
    voc_across(0).wait_recv()
    voc_across(1).wait_recv()
    for dy in range(1, DP):
        voc_along(dy, dp).start()
    own_copy.wait()
    for copy in loads[1:4]:
        copy.wait()
    for group in range(GROUPS):
        low, high = (max(1, group * per_group), (group + 1) * per_group)

        @pl.loop(low, high)
        def _(i):
            out(i).wait_recv()

        @pl.loop(0, local)
        def _(n):
            inputs = arrived[n, pl.ds(group * chunk, chunk)]
            gate_part = jnp.dot(inputs, gate_w[n], preferred_element_type=jnp.float32)
            up_part = jnp.dot(inputs, up_w[n], preferred_element_type=jnp.float32)
            active = (jax.nn.silu(gate_part) * up_part).astype(jnp.bfloat16)
            result[n, pl.ds(group * chunk, chunk)] = jnp.dot(active, down_w[n], preferred_element_type=jnp.float32).astype(jnp.bfloat16)
        if group == 0:
            home = pltpu.make_async_copy(result.at[:, pl.ds(0, slots)], returned.at[0], self_sem)
            home.start()

        @pl.loop(low, high)
        def _(i):
            back(i).start()
    for dy in range(DP):
        source = (dp + DP - dy) % DP
        if dy:
            voc_along(dy, source).wait_recv()

        @pl.loop(0, quarter // 128)
        def _(j):
            start = source * quarter + j * 128
            vocab_t[pl.ds(pl.multiple_of(voc + start, 128), 128), :] = other_raw[:, pl.ds(pl.multiple_of(start, 128), 128)].T
    above = x * 8 + (z + 1) % SIDE * 2 + core
    below = x * 8 + (z + SIDE - 1) % SIDE * 2 + core
    mate = mate_x * 8 + z * 2 + core
    sibling = x * 8 + z * 2 + 1 - core
    sends = []

    def row_copy(slot, h, there, device, side=0):
        number = len(sends)

        def made():
            return remote(rows.at[slot, h, 0], rows.at[there, h, side], send_rows.at[number], recv_rows.at[(there * 2 + h) * 2 + side], at(device))
        sends.append(made)
        return made

    def row_arrival(slot, h, side):
        return remote(rows.at[slot, h, side], rows.at[slot, h, side], send_rows.at[0], recv_rows.at[(slot * 2 + h) * 2 + side], at(sibling))
    copies = {}
    moves = [move for moves in (FIRST_SENDS, *(entry[1:] for entry in SCHEDULE)) for move in moves if len(move) == 3]
    for slot, h, way in moves:
        jx, jz = (slot // SIDE, slot % SIDE)
        if way == ABOVE:
            copies[slot, h, way] = row_copy(slot, h, jx * SIDE + (jz + 3) % SIDE, above)
        elif way == BELOW:
            copies[slot, h, way] = row_copy(slot, h, jx * SIDE + (jz + 1) % SIDE, below)
        elif way == MATE:
            copies[slot, h, way] = row_copy(slot, h, (1 - jx) * SIDE + jz, mate)
        else:
            copies[slot, h, way] = row_copy(slot, h, slot, sibling, 1)
    home.wait()
    mixed[...] = hidden[...].astype(jnp.float32)
    for group in range(GROUPS):
        low, high = (max(1, group * per_group), (group + 1) * per_group)

        @pl.loop(low, high)
        def _(i):
            back(i).wait_recv()
        block = returned[pl.ds(group * per_group, per_group)].reshape(per_group * part, width)
        span = slice(group * per_group * part, (group + 1) * per_group * part)

        def add(lines):
            return mixed[lines, :] + (gate_a[lines] * jnp.dot(place_a[lines, span], block, preferred_element_type=jnp.float32) + gate_b[lines] * jnp.dot(place_b[lines, span], block, preferred_element_type=jnp.float32))
        if group < GROUPS - 1:
            mixed[...] = add(slice(0, tokens))
        else:
            for h in range(2):
                lines = slice(h * half, (h + 1) * half)
                rows[0, h, 0] = normalize(add(lines), final_gain_ref[...]).astype(jnp.bfloat16)
                for move in FIRST_SENDS:
                    if move[1] == h:
                        copies[move]().start()

    @pl.loop(1, PEERS)
    def _(q):
        target_copy(seen_from(q)).wait_recv()
    own_base = own * voc
    other_base = mirror * voc
    tile = voc // 2

    def stats_copy(q):
        there = seen_from(q)
        return remote(stats_out.at[q], stats_in.at[there], send_stats.at[q], recv_stats.at[there], at(peer(q)))

    @pl.loop(0, PEERS)
    def _(q):
        stats_out[q] = jnp.zeros(stats_out.shape[1:], jnp.float32)

    @pl.loop(0, len(SCHEDULE))
    def _(step):
        slot = looked_up([entry[0][0] for entry in SCHEDULE], step)
        h = looked_up([entry[0][1] for entry in SCHEDULE], step)
        for k, entry in enumerate(SCHEDULE):
            if len(entry) == 1:
                continue

            @pl.when(step == k)
            def _():
                for move in entry[1:]:
                    if len(move) == 2:
                        row_arrival(*move, 0).wait_recv()
                    else:
                        copies[move]().start()
        row_arrival(slot, h, 1).wait_recv()
        block = rows[slot, h].reshape(2 * half, width)
        wanted = jnp.concatenate([targets[2 * slot, pl.ds(h, 1), :], targets[2 * slot + 1, pl.ds(h, 1), :]], axis=1)
        high = total = hit = None
        for n in range(4):
            scores = lax.dot_general(vocab_t[n * tile:(n + 1) * tile, :], block, (((1,), (1,)), ((), ())), preferred_element_type=jnp.float32)
            base = (own_base if n < 2 else other_base) + n % 2 * tile
            match = lax.broadcasted_iota(jnp.int32, scores.shape, 0) == wanted - base
            stacked = scores.reshape(tile // 8, 8, 2 * half)
            found = jnp.sum(jnp.where(match, scores, 0.0).reshape(stacked.shape), axis=0)
            top = jnp.max(stacked, axis=0)
            if n:
                top = jnp.maximum(top, high)
            summed = jnp.sum(jnp.exp(stacked - top[None]), axis=0)
            if n:
                summed = summed + total * jnp.exp(high - top)
                found = found + hit
            high, total, hit = (top, summed, found)
        top = jnp.max(high, axis=0, keepdims=True)
        summed = jnp.sum(total * jnp.exp(high - top), axis=0, keepdims=True)
        found = jnp.sum(hit, axis=0, keepdims=True)
        for side in range(2):
            lanes = slice(side * half, (side + 1) * half)
            stats_out[2 * slot + side, pl.ds(h, 1), :] = top[:, lanes]
            stats_out[2 * slot + side, pl.ds(2 + h, 1), :] = summed[:, lanes]
            stats_out[2 * slot + side, pl.ds(4 + h, 1), :] = found[:, lanes]
        last = looked_up([int(all((e[0] != entry[0] and e[0][0] != entry[0][0] for e in SCHEDULE[k + 1:]))) for k, entry in enumerate(SCHEDULE)], step)

        @pl.when(last == 1)
        def _():

            @pl.when(slot > 0)
            def _():
                stats_copy(2 * slot).start()
            stats_copy(2 * slot + 1).start()
    stats_in[0] = stats_out[0]

    @pl.loop(1, PEERS)
    def _(q):
        stats_copy(seen_from(q)).wait_recv()
    every = stats_in[...]
    top = jnp.max(every[:, 0:2], axis=0)
    summed = jnp.sum(every[:, 2:4] * jnp.exp(every[:, 0:2] - top[None]), axis=0)
    found = jnp.sum(every[:, 4:6], axis=0)
    docs = docs_ref[...]
    two_rows = lax.broadcasted_iota(jnp.int32, docs.shape, 0)
    two_lanes = lax.broadcasted_iota(jnp.int32, docs.shape, 1)
    at_end = (two_rows == 1) & (two_lanes == half - 1) & (linear == devices - 1)
    counted = (targets[0, 2:4, :] == docs) & jnp.logical_not(at_end)
    token_loss = jnp.where(counted, top + jnp.log(summed) - found, 0.0)
    made_ref[0:2, :] = token_loss

    def whole(values):
        return jnp.sum(jnp.sum(values, axis=1, keepdims=True), axis=0, keepdims=True)

    def of_document(number):
        mask = docs == number
        return (whole(jnp.where(mask, token_loss, 0.0)), whole(jnp.where(mask, 1.0, 0.0)))
    lead_loss, lead_length = of_document(DOC_DEV * linear - 1)
    lines = lax.broadcasted_iota(jnp.int32, (8, 128), 0)
    sums_out[...] = jnp.where(lines == 0, whole(token_loss), jnp.where(lines == 1, lead_loss, jnp.where(lines == 2, lead_length, 0.0)))

    def sum_copy(q):
        there = seen_from(q)
        return remote(sums_out, sums_in.at[there], send_sums.at[q], recv_sums.at[there], at(peer(q)))

    def wide_copy(i):
        device, plane = across(i)
        return remote(wide_out, wide_in.at[i], send_wide.at[i], recv_wide.at[i], at(device, plane))

    def lead_copy():
        return remote(sums_out, lead_in, send_lead, recv_lead, shifted(-1))
    for q in range(1, PEERS):
        sum_copy(q).start()
    lead_copy().start()
    sums_in[0] = sums_out[...]
    parts = [of_document(DOC_DEV * linear + j) for j in range(DOC_DEV)]
    for q in range(1, PEERS):
        sum_copy(seen_from(q)).wait_recv()
    wide_out[...] = jnp.sum(sums_in[...], axis=0)
    for i in range(1, 2 * DP):
        wide_copy(i).start()
    wide_in[0] = wide_out[...]
    lead_copy().wait_recv()
    for i in range(1, 2 * DP):
        wide_copy(i).wait_recv()
    global_sum = jnp.sum(wide_in[...], axis=0)[0:1, 0:1]
    global_mean = global_sum / (tokens * devices - DOC_DEV * devices)
    lanes = lax.broadcasted_iota(jnp.int32, (1, 128), 1)
    scores = jnp.zeros((1, 128), jnp.float32)
    for j, (part_loss, part_length) in enumerate(parts):
        if j == DOC_DEV - 1:
            part_loss = part_loss + lead_in[1:2, 0:1]
            part_length = part_length + lead_in[2:3, 0:1]
        scores = jnp.where(lanes == j, part_loss / part_length - global_mean, scores)
    made_ref[2:3, :] = scores

    @pl.loop(1, OWNERS)
    def _(i):
        out(i).wait_send()
        back(i).wait_send()

    @pl.loop(1, PEERS)
    def _(q):
        target_copy(q).wait_send()
        stats_copy(q).wait_send()
    voc_across(0).wait_send()
    voc_across(1).wait_send()
    ids_copy().wait_send()
    lead_copy().wait_send()
    for q in range(1, PEERS):
        sum_copy(q).wait_send()
    for i in range(1, 2 * DP):
        wide_copy(i).wait_send()
    for dy in range(1, DP):
        voc_along(dy, dp).wait_send()
    for made in sends:
        made().wait_send()

def local(hidden_in, moe_gain, router_weight, expert_gate, expert_up, expert_down, final_gain, vocab_weight, token_ids, doc_ids, routes):
    tokens, width = hidden_in.shape
    here, _, hidden_units = expert_gate.shape
    voc = vocab_weight.shape[1]
    experts = OWNERS * here
    slots = max(2, 2 * TOP * tokens // experts)
    half = tokens // 2
    bf16, f32, i32 = (jnp.bfloat16, jnp.float32, jnp.int32)
    vmem = pl.BlockSpec(memory_space=pltpu.VMEM)
    hbm = pl.BlockSpec(memory_space=pl.ANY)
    dma = pltpu.SemaphoreType.DMA
    made = pl.pallas_call(kernel, out_shape=jax.ShapeDtypeStruct((8, half), f32), in_specs=[hbm] + [vmem] * 6 + [hbm] * 4, out_specs=vmem, scratch_shapes=[pltpu.VMEM((tokens, width), bf16), pltpu.VMEM((tokens, width), bf16), pltpu.VMEM((OWNERS, here, slots, width), bf16), pltpu.VMEM((here, OWNERS * slots, width), bf16), pltpu.VMEM((here, width, hidden_units), bf16), pltpu.VMEM((here, width, hidden_units), bf16), pltpu.VMEM((here, hidden_units, width), bf16), pltpu.VMEM((here, OWNERS * slots, width), bf16), pltpu.VMEM((OWNERS, here, slots, width), bf16), pltpu.VMEM((tokens, experts * slots), bf16), pltpu.VMEM((tokens, experts * slots), bf16), pltpu.VMEM((tokens, width), f32), pltpu.VMEM((width, voc), bf16), pltpu.VMEM((width, voc), bf16), pltpu.VMEM((2 * voc, width), bf16), pltpu.VMEM((8, 2, 2, half, width), bf16), pltpu.VMEM((8, half), i32), pltpu.VMEM((8, half), i32), pltpu.VMEM((PEERS, 8, half), i32), pltpu.VMEM((PEERS, 8, half), f32), pltpu.VMEM((PEERS, 8, half), f32), pltpu.VMEM((8, 128), f32), pltpu.VMEM((PEERS, 8, 128), f32), pltpu.VMEM((8, 128), f32), pltpu.VMEM((8, 128), f32), pltpu.VMEM((2 * DP, 8, 128), f32), dma((5,)), dma, dma((OWNERS,)), dma((OWNERS,)), dma((OWNERS,)), dma((OWNERS,)), dma((DP + 1,)), dma((DP + 1,)), dma, dma, dma((PEERS,)), dma((PEERS,)), dma((32,)), dma((32,)), dma((PEERS,)), dma((PEERS,)), dma((PEERS,)), dma((PEERS,)), dma, dma, dma((2 * DP,)), dma((2 * DP,))], compiler_params=pltpu.CompilerParams(collective_id=0, has_side_effects=True, vmem_limit_bytes=58 * 2 ** 20), name='scoring')(hidden_in, moe_gain.reshape(1, width), router_weight.T, routes.T, final_gain.reshape(1, width), token_ids.reshape(2, half), doc_ids.reshape(2, half), expert_gate, expert_up, expert_down, vocab_weight)
    return (made[0:2].reshape(tokens), made[2, :DOC_DEV])

def solution(mesh):
    in_specs = (P(BOTH, None), P(), P(), P('expert', None, None), P('expert', None, None), P('expert', None, None), P(), P(None, 'expert'), P(BOTH), P(BOTH), P(BOTH, None))
    return jax.shard_map(local, mesh=mesh, in_specs=in_specs, out_specs=(P(BOTH), P(BOTH)), check_vma=False)
```

```python
import jax
import jax.numpy as jnp
from jax import lax
from jax.experimental import pallas as pl
from jax.experimental.pallas import tpu as pltpu
from jax.sharding import PartitionSpec as P
TOP = 2
DOC_DEV = 4
SIDE = 4
DP = 4
OWNERS = 32
GROUPS = 4
PEERS = 16
BOTH = ('dp', 'expert')
ABOVE, BELOW, MATE, SIBLING = ("above", "below", "mate", "sibling")
FIRST_SENDS = (
    (0, 0, ABOVE), (0, 0, BELOW), (0, 0, MATE), (0, 0, SIBLING), (0, 1, ABOVE), (0, 1, BELOW), (0, 1, MATE), (0, 1, SIBLING),
)
SCHEDULE = (
    ((0, 0), (1, 0), (4, 0), (1, 0, BELOW), (4, 0, SIBLING), (1, 0, MATE), (4, 0, ABOVE),),
    ((4, 0),),
    ((0, 1),),
    ((4, 1), (1, 1), (4, 1), (1, 1, SIBLING), (3, 1), (1, 1, BELOW), (3, 0), (4, 1, SIBLING), (3, 1, MATE), (4, 1, BELOW), (3, 1, SIBLING),),
    ((1, 1),),
    ((3, 1), (5, 0), (3, 0, SIBLING), (7, 0), (7, 0, ABOVE), (1, 0, SIBLING), (7, 0, SIBLING), (5, 0, SIBLING),),
    ((7, 0),),
    ((3, 0), (2, 0), (2, 0, SIBLING),),
    ((2, 0), (2, 1), (2, 1, MATE), (7, 1), (2, 1, SIBLING),),
    ((1, 0),),
    ((5, 0), (6, 0),),
    ((2, 1), (6, 0, SIBLING),),
    ((6, 0), (7, 1, SIBLING), (5, 1),),
    ((7, 1), (6, 1), (5, 1, SIBLING), (6, 1, SIBLING),),
    ((6, 1),),
    ((5, 1),),
)
EPSILON = 1e-06

def each(low, high):

    def over(body):
        for i in range(low, high):
            body(i)
    return over
MESH_ID = pl.DeviceIdType.MESH
EPSILON = 1e-06

def normalize(values, gain_vector):
    inv_scale = lax.rsqrt(jnp.mean(values * values, axis=-1, keepdims=True) + EPSILON)
    return values * inv_scale * gain_vector

def looked_up(table, step):
    found = jnp.int32(table[0])
    for k in range(1, len(table)):
        found = jnp.where(step == k, jnp.int32(table[k]), found)
    return found

def kernel(hidden_hbm, gain_ref, router_ref, routes_ref, final_gain_ref, tokens_ref, docs_ref, gate_hbm, up_hbm, down_hbm, vocab_hbm, made_ref, hidden, normed, outgoing, arrived, gate_w, up_w, down_w, result, returned, place_a, place_b, mixed, own_raw, other_raw, vocab_t, rows, ids, next_ids, targets, stats_out, stats_in, sums_out, sums_in, lead_in, wide_out, wide_in, load_sem, self_sem, send_out, recv_out, send_back, recv_back, send_voc, recv_voc, send_ids, recv_ids, send_tgt, recv_tgt, send_rows, recv_rows, send_stats, recv_stats, send_sums, recv_sums, send_lead, recv_lead, send_wide, recv_wide):
    tokens, width = hidden.shape
    local = gate_hbm.shape[0]
    experts = OWNERS * local
    slots = outgoing.shape[2]
    part = local * slots
    per_group = OWNERS // GROUPS
    chunk = per_group * slots
    voc = vocab_hbm.shape[1]
    quarter = voc // DP
    half = tokens // 2
    dp = lax.axis_index('dp')
    own = lax.axis_index('expert')
    x, z, core = (own // 8, own // 2 % SIDE, own % 2)
    linear = dp * OWNERS + own
    devices = DP * OWNERS
    mate_x = x + 1 - 2 * (x % 2)
    mirror = (SIDE - 1 - x) * 8 + z * 2 + core

    def at(device, plane=dp):
        return {'dp': plane, 'expert': device}

    def shifted(steps):
        other = (linear + steps + devices) % devices
        return at(other % OWNERS, other // OWNERS)
    x_part = [(x + d) % SIDE * 8 for d in range(SIDE)]
    z_part = [(z + d) % SIDE * 2 for d in range(SIDE)]
    c_part = [core, 1 - core]

    def partner(i, sign):
        dx, dc, k = (i % 4, i // 16, i // 4 % 4)
        dz = (k + SIDE - dx) % SIDE
        if isinstance(i, int):
            return x_part[sign * dx % SIDE] + z_part[sign * dz % SIDE] + c_part[dc]
        return (x + sign * dx + SIDE) % SIDE * 8 + (z + sign * dz + SIDE) % SIDE * 2 + (core + dc) % 2

    def peer(q):
        jx, jz, jc = (q // 8, q // 2 % SIDE, q % 2)
        if isinstance(q, int):
            return (mate_x if jx else x) * 8 + z_part[jz] + c_part[jc]
        return (x + jx * (mate_x - x)) * 8 + (z + jz) % SIDE * 2 + (core + jc) % 2

    def seen_from(q):
        return q // 8 * 8 + (SIDE - q // 2 % SIDE) % SIDE * 2 + q % 2

    def across(i):
        return (own if i % 2 == 0 else mirror, (dp + i // 2) % DP)

    def remote(source, target, send, recv, device):
        return pltpu.make_async_remote_copy(src_ref=source, dst_ref=target, send_sem=send, recv_sem=recv, device_id=device, device_id_type=MESH_ID)
    barrier = pltpu.get_barrier_semaphore()

    @each(1, OWNERS)
    def _(i):
        pl.semaphore_signal(barrier, inc=1, device_id=at(partner(i, 1)), device_id_type=MESH_ID)
    for i in range(2, 2 * DP):
        device, plane = across(i)
        pl.semaphore_signal(barrier, inc=1, device_id=at(device, plane), device_id_type=MESH_ID)
    for steps in (-1, 1):
        pl.semaphore_signal(barrier, inc=1, device_id=shifted(steps), device_id_type=MESH_ID)
    loads = []
    for n, (source, target) in enumerate(((hidden_hbm, hidden), (gate_hbm, gate_w), (up_hbm, up_w), (down_hbm, down_w), (vocab_hbm, own_raw))):
        copy = pltpu.make_async_copy(source, target, load_sem.at[n])
        copy.start()
        loads.append(copy)
    ids[...] = jnp.zeros_like(ids)
    ids[0:2, :] = tokens_ref[...]
    ids[2:4, :] = docs_ref[...]
    pl.semaphore_wait(barrier, OWNERS - 1 + 2 * (DP - 1) + 2)

    def columns(plane):
        return pl.ds(pl.multiple_of(plane * quarter, quarter), quarter)

    def voc_across(piece):
        span = pl.ds(pl.multiple_of(dp * quarter + piece * (quarter // 2), quarter // 2), quarter // 2)
        n = piece * DP
        return remote(vocab_hbm.at[:, span], other_raw.at[:, span], send_voc.at[n], recv_voc.at[n], at(mirror))

    def voc_along(dy, source):
        return remote(other_raw.at[:, columns(source)], other_raw.at[:, columns(source)], send_voc.at[dy], recv_voc.at[dy], at(own, (dp + dy) % DP))

    def ids_copy():
        return remote(ids, next_ids, send_ids, recv_ids, shifted(-1))
    ids_copy().start()
    for piece in range(2):
        voc_across(piece).start()
    loads[0].wait()
    normed[...] = normalize(hidden[...].astype(jnp.float32), gain_ref[...]).astype(jnp.bfloat16)
    first = routes_ref[0:1, :]
    second = routes_ref[1:2, :]
    expert_iota = lax.broadcasted_iota(jnp.int32, (experts, tokens), 0)
    is_first = expert_iota == first
    is_second = expert_iota == second
    member = jnp.where(is_first | is_second, 1.0, 0.0).astype(jnp.bfloat16)
    earlier = lax.broadcasted_iota(jnp.int32, (tokens, tokens), 0) < lax.broadcasted_iota(jnp.int32, (tokens, tokens), 1)
    rank = jnp.dot(member, jnp.where(earlier, 1.0, 0.0).astype(jnp.bfloat16), preferred_element_type=jnp.float32)

    def position(expert, chosen):
        owner = expert // local
        dx = (owner // 8 + SIDE - x) % SIDE
        dz = (owner // 2 % SIDE + SIDE - z) % SIDE
        dc = (owner + core) % 2
        k = (dx + dz) % SIDE
        index = dc * 16 + k * 4 + dx
        own_rank = jnp.sum(jnp.where(chosen, rank, 0.0), axis=0, keepdims=True).astype(jnp.int32)
        return index * part + expert % local * slots + own_rank
    first_pos = position(first, is_first)
    second_pos = position(second, is_second)

    def slot_rows(i):
        return pl.ds(i * slots if isinstance(i, int) else pl.multiple_of(i * slots, slots), slots)

    def out(i):
        return remote(outgoing.at[i], arrived.at[:, slot_rows(i)], send_out.at[i], recv_out.at[i], at(partner(i, 1)))

    def back(i):
        return remote(result.at[:, slot_rows(i)], returned.at[i], send_back.at[i], recv_back.at[i], at(partner(i, -1)))
    for group in range(GROUPS):
        slot_iota = lax.broadcasted_iota(jnp.int32, (per_group * part, tokens), 0) + group * per_group * part
        chosen = (slot_iota == first_pos) | (slot_iota == second_pos)
        block = jnp.dot(jnp.where(chosen, 1.0, 0.0).astype(jnp.bfloat16), normed[...], preferred_element_type=jnp.float32)
        outgoing[pl.ds(group * per_group, per_group)] = block.astype(jnp.bfloat16).reshape(per_group, local, slots, width)
        if group == 0:
            own_copy = pltpu.make_async_copy(outgoing.at[0], arrived.at[:, pl.ds(0, slots)], self_sem)
            own_copy.start()

        @each(max(1, group * per_group), (group + 1) * per_group)
        def _(i):
            out(i).start()
    ids_copy().wait_recv()
    row_iota = lax.broadcasted_iota(jnp.int32, ids.shape, 0)
    lane_iota = lax.broadcasted_iota(jnp.int32, ids.shape, 1)
    own_ids = ids[...]
    after = pltpu.roll(own_ids, half - 1, 1)
    ends = lane_iota == half - 1
    after = jnp.where(ends & (row_iota == 0), own_ids[1:2, 0:1], after)
    after = jnp.where(ends & (row_iota == 1), next_ids[0:1, 0:1], after)
    after = jnp.where(ends & (row_iota == 2), own_ids[3:4, 0:1], after)
    after = jnp.where(ends & (row_iota == 3), next_ids[2:3, 0:1], after)
    targets[0] = after

    def target_copy(q):
        there = seen_from(q)
        return remote(targets.at[0], targets.at[there], send_tgt.at[q], recv_tgt.at[there], at(peer(q)))

    @each(1, PEERS)
    def _(q):
        target_copy(q).start()
    router_scores = lax.dot_general(router_ref[...], normed[...], (((1,), (1,)), ((), ())), preferred_element_type=jnp.float32)
    picked = jnp.sum(jnp.where(is_first, router_scores, 0.0) - jnp.where(is_second, router_scores, 0.0), axis=0, keepdims=True)
    first_gate = jax.nn.sigmoid(picked)
    lines = lax.broadcasted_iota(jnp.int32, (128, tokens), 0)
    table = jnp.where(lines == 0, first_pos.astype(jnp.float32), jnp.where(lines == 1, second_pos.astype(jnp.float32), jnp.where(lines == 2, first_gate, 0.0)))
    per_token = table.T
    place_iota = lax.broadcasted_iota(jnp.int32, (tokens, experts * slots), 1).astype(jnp.float32)
    place_a[...] = jnp.where(place_iota == per_token[:, 0:1], 1.0, 0.0).astype(jnp.bfloat16)
    place_b[...] = jnp.where(place_iota == per_token[:, 1:2], 1.0, 0.0).astype(jnp.bfloat16)
    gate_a = per_token[:, 2:3]
    gate_b = 1.0 - gate_a
    loads[4].wait()

    @pl.loop(0, voc // 128)
    def _(j):
        strip = pl.ds(pl.multiple_of(j * 128, 128), 128)
        vocab_t[strip, :] = own_raw[:, strip].T
    voc_across(0).wait_recv()
    voc_across(1).wait_recv()
    for dy in range(1, DP):
        voc_along(dy, dp).start()
    own_copy.wait()
    for copy in loads[1:4]:
        copy.wait()
    for group in range(GROUPS):
        low, high = (max(1, group * per_group), (group + 1) * per_group)

        @each(low, high)
        def _(i):
            out(i).wait_recv()

        @pl.loop(0, local)
        def _(n):
            inputs = arrived[n, pl.ds(group * chunk, chunk)]
            gate_part = jnp.dot(inputs, gate_w[n], preferred_element_type=jnp.float32)
            up_part = jnp.dot(inputs, up_w[n], preferred_element_type=jnp.float32)
            active = (jax.nn.silu(gate_part) * up_part).astype(jnp.bfloat16)
            result[n, pl.ds(group * chunk, chunk)] = jnp.dot(active, down_w[n], preferred_element_type=jnp.float32).astype(jnp.bfloat16)
        if group == 0:
            home = pltpu.make_async_copy(result.at[:, pl.ds(0, slots)], returned.at[0], self_sem)
            home.start()

        @each(low, high)
        def _(i):
            back(i).start()
    for dy in range(DP):
        source = (dp + DP - dy) % DP
        if dy:
            voc_along(dy, source).wait_recv()

        @pl.loop(0, quarter // 128)
        def _(j):
            start = source * quarter + j * 128
            vocab_t[pl.ds(pl.multiple_of(voc + start, 128), 128), :] = other_raw[:, pl.ds(pl.multiple_of(start, 128), 128)].T
    above = x * 8 + (z + 1) % SIDE * 2 + core
    below = x * 8 + (z + SIDE - 1) % SIDE * 2 + core
    mate = mate_x * 8 + z * 2 + core
    sibling = x * 8 + z * 2 + 1 - core
    sends = []

    def row_copy(slot, h, there, device, side=0):
        number = len(sends)

        def made():
            return remote(rows.at[slot, h, 0], rows.at[there, h, side], send_rows.at[number], recv_rows.at[(there * 2 + h) * 2 + side], at(device))
        sends.append(made)
        return made

    def row_arrival(slot, h, side):
        return remote(rows.at[slot, h, side], rows.at[slot, h, side], send_rows.at[0], recv_rows.at[(slot * 2 + h) * 2 + side], at(sibling))
    copies = {}
    moves = [move for moves in (FIRST_SENDS, *(entry[1:] for entry in SCHEDULE)) for move in moves if len(move) == 3]
    for slot, h, way in moves:
        jx, jz = (slot // SIDE, slot % SIDE)
        if way == ABOVE:
            copies[slot, h, way] = row_copy(slot, h, jx * SIDE + (jz + 3) % SIDE, above)
        elif way == BELOW:
            copies[slot, h, way] = row_copy(slot, h, jx * SIDE + (jz + 1) % SIDE, below)
        elif way == MATE:
            copies[slot, h, way] = row_copy(slot, h, (1 - jx) * SIDE + jz, mate)
        else:
            copies[slot, h, way] = row_copy(slot, h, slot, sibling, 1)
    home.wait()
    mixed[...] = hidden[...].astype(jnp.float32)
    for group in range(GROUPS):
        low, high = (max(1, group * per_group), (group + 1) * per_group)

        @each(low, high)
        def _(i):
            back(i).wait_recv()
        block = returned[pl.ds(group * per_group, per_group)].reshape(per_group * part, width)
        span = slice(group * per_group * part, (group + 1) * per_group * part)

        def add(lines):
            return mixed[lines, :] + (gate_a[lines] * jnp.dot(place_a[lines, span], block, preferred_element_type=jnp.float32) + gate_b[lines] * jnp.dot(place_b[lines, span], block, preferred_element_type=jnp.float32))
        if group < GROUPS - 1:
            mixed[...] = add(slice(0, tokens))
        else:
            for h in range(2):
                lines = slice(h * half, (h + 1) * half)
                rows[0, h, 0] = normalize(add(lines), final_gain_ref[...]).astype(jnp.bfloat16)
                for move in FIRST_SENDS:
                    if move[1] == h:
                        copies[move]().start()

    @each(1, PEERS)
    def _(q):
        target_copy(seen_from(q)).wait_recv()
    own_base = own * voc
    other_base = mirror * voc
    tile = voc

    def stats_copy(q):
        there = seen_from(q)
        return remote(stats_out.at[q], stats_in.at[there], send_stats.at[q], recv_stats.at[there], at(peer(q)))

    @pl.loop(0, PEERS)
    def _(q):
        stats_out[q] = jnp.zeros(stats_out.shape[1:], jnp.float32)

    @pl.loop(0, len(SCHEDULE))
    def _(step):
        slot = looked_up([entry[0][0] for entry in SCHEDULE], step)
        h = looked_up([entry[0][1] for entry in SCHEDULE], step)
        for k, entry in enumerate(SCHEDULE):
            if len(entry) == 1:
                continue

            @pl.when(step == k)
            def _():
                for move in entry[1:]:
                    if len(move) == 2:
                        row_arrival(*move, 0).wait_recv()
                    else:
                        copies[move]().start()
        row_arrival(slot, h, 1).wait_recv()
        block = rows[slot, h].reshape(2 * half, width)
        wanted = jnp.concatenate([targets[2 * slot, pl.ds(h, 1), :], targets[2 * slot + 1, pl.ds(h, 1), :]], axis=1)
        high = total = hit = None
        for n in range(2):
            scores = lax.dot_general(vocab_t[n * tile:(n + 1) * tile, :], block, (((1,), (1,)), ((), ())), preferred_element_type=jnp.float32)
            base = own_base if n == 0 else other_base
            match = lax.broadcasted_iota(jnp.int32, scores.shape, 0) == wanted - base
            stacked = scores.reshape(tile // 8, 8, 2 * half)
            found = jnp.sum(jnp.where(match, scores, 0.0).reshape(stacked.shape), axis=0)
            top = jnp.max(stacked, axis=0)
            if n:
                top = jnp.maximum(top, high)
            summed = jnp.sum(jnp.exp(stacked - top[None]), axis=0)
            if n:
                summed = summed + total * jnp.exp(high - top)
                found = found + hit
            high, total, hit = (top, summed, found)
        top = jnp.max(high, axis=0, keepdims=True)
        summed = jnp.sum(total * jnp.exp(high - top), axis=0, keepdims=True)
        found = jnp.sum(hit, axis=0, keepdims=True)
        for side in range(2):
            lanes = slice(side * half, (side + 1) * half)
            stats_out[2 * slot + side, pl.ds(h, 1), :] = top[:, lanes]
            stats_out[2 * slot + side, pl.ds(2 + h, 1), :] = summed[:, lanes]
            stats_out[2 * slot + side, pl.ds(4 + h, 1), :] = found[:, lanes]
        last = looked_up([int(all((e[0] != entry[0] and e[0][0] != entry[0][0] for e in SCHEDULE[k + 1:]))) for k, entry in enumerate(SCHEDULE)], step)

        @pl.when(last == 1)
        def _():

            @pl.when(slot > 0)
            def _():
                stats_copy(2 * slot).start()
            stats_copy(2 * slot + 1).start()
    stats_in[0] = stats_out[0]

    @each(1, PEERS)
    def _(q):
        stats_copy(seen_from(q)).wait_recv()
    every = stats_in[...]
    top = jnp.max(every[:, 0:2], axis=0)
    summed = jnp.sum(every[:, 2:4] * jnp.exp(every[:, 0:2] - top[None]), axis=0)
    found = jnp.sum(every[:, 4:6], axis=0)
    docs = docs_ref[...]
    two_rows = lax.broadcasted_iota(jnp.int32, docs.shape, 0)
    two_lanes = lax.broadcasted_iota(jnp.int32, docs.shape, 1)
    at_end = (two_rows == 1) & (two_lanes == half - 1) & (linear == devices - 1)
    counted = (targets[0, 2:4, :] == docs) & jnp.logical_not(at_end)
    token_loss = jnp.where(counted, top + jnp.log(summed) - found, 0.0)
    made_ref[0:2, :] = token_loss

    def whole(values):
        return jnp.sum(jnp.sum(values, axis=1, keepdims=True), axis=0, keepdims=True)

    def of_document(number):
        mask = docs == number
        return (whole(jnp.where(mask, token_loss, 0.0)), whole(jnp.where(mask, 1.0, 0.0)))
    lead_loss, lead_length = of_document(DOC_DEV * linear - 1)
    lines = lax.broadcasted_iota(jnp.int32, (8, 128), 0)
    sums_out[...] = jnp.where(lines == 0, whole(token_loss), jnp.where(lines == 1, lead_loss, jnp.where(lines == 2, lead_length, 0.0)))

    def sum_copy(q):
        there = seen_from(q)
        return remote(sums_out, sums_in.at[there], send_sums.at[q], recv_sums.at[there], at(peer(q)))

    def wide_copy(i):
        device, plane = across(i)
        return remote(wide_out, wide_in.at[i], send_wide.at[i], recv_wide.at[i], at(device, plane))

    def lead_copy():
        return remote(sums_out, lead_in, send_lead, recv_lead, shifted(-1))
    for q in range(1, PEERS):
        sum_copy(q).start()
    lead_copy().start()
    sums_in[0] = sums_out[...]
    parts = [of_document(DOC_DEV * linear + j) for j in range(DOC_DEV)]
    for q in range(1, PEERS):
        sum_copy(seen_from(q)).wait_recv()
    wide_out[...] = jnp.sum(sums_in[...], axis=0)
    for i in range(1, 2 * DP):
        wide_copy(i).start()
    wide_in[0] = wide_out[...]
    lead_copy().wait_recv()
    for i in range(1, 2 * DP):
        wide_copy(i).wait_recv()
    global_sum = jnp.sum(wide_in[...], axis=0)[0:1, 0:1]
    global_mean = global_sum / (tokens * devices - DOC_DEV * devices)
    lanes = lax.broadcasted_iota(jnp.int32, (1, 128), 1)
    scores = jnp.zeros((1, 128), jnp.float32)
    for j, (part_loss, part_length) in enumerate(parts):
        if j == DOC_DEV - 1:
            part_loss = part_loss + lead_in[1:2, 0:1]
            part_length = part_length + lead_in[2:3, 0:1]
        scores = jnp.where(lanes == j, part_loss / part_length - global_mean, scores)
    made_ref[2:3, :] = scores

    @each(1, OWNERS)
    def _(i):
        out(i).wait_send()
        back(i).wait_send()

    @each(1, PEERS)
    def _(q):
        target_copy(q).wait_send()
        stats_copy(q).wait_send()
    voc_across(0).wait_send()
    voc_across(1).wait_send()
    ids_copy().wait_send()
    lead_copy().wait_send()
    for q in range(1, PEERS):
        sum_copy(q).wait_send()
    for i in range(1, 2 * DP):
        wide_copy(i).wait_send()
    for dy in range(1, DP):
        voc_along(dy, dp).wait_send()
    for made in sends:
        made().wait_send()

def local(hidden_in, moe_gain, router_weight, expert_gate, expert_up, expert_down, final_gain, vocab_weight, token_ids, doc_ids, routes):
    tokens, width = hidden_in.shape
    here, _, hidden_units = expert_gate.shape
    voc = vocab_weight.shape[1]
    experts = OWNERS * here
    slots = max(2, 2 * TOP * tokens // experts)
    half = tokens // 2
    bf16, f32, i32 = (jnp.bfloat16, jnp.float32, jnp.int32)
    vmem = pl.BlockSpec(memory_space=pltpu.VMEM)
    hbm = pl.BlockSpec(memory_space=pl.ANY)
    dma = pltpu.SemaphoreType.DMA
    made = pl.pallas_call(kernel, out_shape=jax.ShapeDtypeStruct((8, half), f32), in_specs=[hbm] + [vmem] * 6 + [hbm] * 4, out_specs=vmem, scratch_shapes=[pltpu.VMEM((tokens, width), bf16), pltpu.VMEM((tokens, width), bf16), pltpu.VMEM((OWNERS, here, slots, width), bf16), pltpu.VMEM((here, OWNERS * slots, width), bf16), pltpu.VMEM((here, width, hidden_units), bf16), pltpu.VMEM((here, width, hidden_units), bf16), pltpu.VMEM((here, hidden_units, width), bf16), pltpu.VMEM((here, OWNERS * slots, width), bf16), pltpu.VMEM((OWNERS, here, slots, width), bf16), pltpu.VMEM((tokens, experts * slots), bf16), pltpu.VMEM((tokens, experts * slots), bf16), pltpu.VMEM((tokens, width), f32), pltpu.VMEM((width, voc), bf16), pltpu.VMEM((width, voc), bf16), pltpu.VMEM((2 * voc, width), bf16), pltpu.VMEM((8, 2, 2, half, width), bf16), pltpu.VMEM((8, half), i32), pltpu.VMEM((8, half), i32), pltpu.VMEM((PEERS, 8, half), i32), pltpu.VMEM((PEERS, 8, half), f32), pltpu.VMEM((PEERS, 8, half), f32), pltpu.VMEM((8, 128), f32), pltpu.VMEM((PEERS, 8, 128), f32), pltpu.VMEM((8, 128), f32), pltpu.VMEM((8, 128), f32), pltpu.VMEM((2 * DP, 8, 128), f32), dma((5,)), dma, dma((OWNERS,)), dma((OWNERS,)), dma((OWNERS,)), dma((OWNERS,)), dma((DP + 1,)), dma((DP + 1,)), dma, dma, dma((PEERS,)), dma((PEERS,)), dma((32,)), dma((32,)), dma((PEERS,)), dma((PEERS,)), dma((PEERS,)), dma((PEERS,)), dma, dma, dma((2 * DP,)), dma((2 * DP,))], compiler_params=pltpu.CompilerParams(collective_id=0, has_side_effects=True, vmem_limit_bytes=58 * 2 ** 20), name='scoring')(hidden_in, moe_gain.reshape(1, width), router_weight.T, routes.T, final_gain.reshape(1, width), token_ids.reshape(2, half), doc_ids.reshape(2, half), expert_gate, expert_up, expert_down, vocab_weight)
    return (made[0:2].reshape(tokens), made[2, :DOC_DEV])

def solution(mesh):
    in_specs = (P(BOTH, None), P(), P(), P('expert', None, None), P('expert', None, None), P('expert', None, None), P(), P(None, 'expert'), P(BOTH), P(BOTH), P(BOTH, None))
    return jax.shard_map(local, mesh=mesh, in_specs=in_specs, out_specs=(P(BOTH), P(BOTH)), check_vma=False)
```

```python
import jax
import jax.numpy as jnp
from jax import lax
from jax.experimental import pallas as pl
from jax.experimental.pallas import tpu as pltpu
from jax.sharding import PartitionSpec as P
TOP = 2
DOC_DEV = 4
SIDE = 4
DP = 4
OWNERS = 32
GROUPS = 4
PEERS = 16
BOTH = ('dp', 'expert')
ABOVE, BELOW, MATE, SIBLING = ("above", "below", "mate", "sibling")
FIRST_SENDS = (
    (0, 0, ABOVE), (0, 0, BELOW), (0, 0, MATE), (0, 0, SIBLING), (0, 1, ABOVE), (0, 1, BELOW), (0, 1, MATE), (0, 1, SIBLING),
)
SCHEDULE = (
    ((0, 0), (1, 0), (4, 0), (1, 0, BELOW), (4, 0, SIBLING), (1, 0, MATE), (4, 0, ABOVE),),
    ((4, 0),),
    ((0, 1),),
    ((4, 1), (1, 1), (4, 1), (1, 1, SIBLING), (3, 1), (1, 1, BELOW), (3, 0), (4, 1, SIBLING), (3, 1, MATE), (4, 1, BELOW), (3, 1, SIBLING),),
    ((1, 1),),
    ((3, 1), (5, 0), (3, 0, SIBLING), (7, 0), (7, 0, ABOVE), (1, 0, SIBLING), (7, 0, SIBLING), (5, 0, SIBLING),),
    ((7, 0),),
    ((3, 0), (2, 0), (2, 0, SIBLING),),
    ((2, 0), (2, 1), (2, 1, MATE), (7, 1), (2, 1, SIBLING),),
    ((1, 0),),
    ((5, 0), (6, 0),),
    ((2, 1), (6, 0, SIBLING),),
    ((6, 0), (7, 1, SIBLING), (5, 1),),
    ((7, 1), (6, 1), (5, 1, SIBLING), (6, 1, SIBLING),),
    ((6, 1),),
    ((5, 1),),
)
EPSILON = 1e-06

def each(low, high):

    def over(body):
        for i in range(low, high):
            body(i)
    return over
MESH_ID = pl.DeviceIdType.MESH
EPSILON = 1e-06

def normalize(values, gain_vector):
    inv_scale = lax.rsqrt(jnp.mean(values * values, axis=-1, keepdims=True) + EPSILON)
    return values * inv_scale * gain_vector

def looked_up(table, step):
    found = jnp.int32(table[0])
    for k in range(1, len(table)):
        found = jnp.where(step == k, jnp.int32(table[k]), found)
    return found

def kernel(hidden_hbm, gain_ref, router_ref, routes_ref, final_gain_ref, tokens_ref, docs_ref, gate_hbm, up_hbm, down_hbm, vocab_hbm, made_ref, hidden, normed, outgoing, arrived, gate_w, up_w, down_w, result, returned, place_a, place_b, mixed, own_raw, other_raw, vocab_t, rows, ids, next_ids, targets, stats_out, stats_in, sums_out, sums_in, lead_in, wide_out, wide_in, load_sem, self_sem, send_out, recv_out, send_back, recv_back, send_voc, recv_voc, send_ids, recv_ids, send_tgt, recv_tgt, send_rows, recv_rows, send_stats, recv_stats, send_sums, recv_sums, send_lead, recv_lead, send_wide, recv_wide):
    tokens, width = hidden.shape
    local = gate_hbm.shape[0]
    experts = OWNERS * local
    slots = outgoing.shape[2]
    part = local * slots
    per_group = OWNERS // GROUPS
    chunk = per_group * slots
    voc = vocab_hbm.shape[1]
    quarter = voc // DP
    half = tokens // 2
    dp = lax.axis_index('dp')
    own = lax.axis_index('expert')
    x, z, core = (own // 8, own // 2 % SIDE, own % 2)
    linear = dp * OWNERS + own
    devices = DP * OWNERS
    mate_x = x + 1 - 2 * (x % 2)
    mirror = (SIDE - 1 - x) * 8 + z * 2 + core

    def at(device, plane=dp):
        return {'dp': plane, 'expert': device}

    def shifted(steps):
        other = (linear + steps + devices) % devices
        return at(other % OWNERS, other // OWNERS)
    x_part = [(x + d) % SIDE * 8 for d in range(SIDE)]
    z_part = [(z + d) % SIDE * 2 for d in range(SIDE)]
    c_part = [core, 1 - core]

    def partner(i, sign):
        dx, dc, k = (i % 4, i // 16, i // 4 % 4)
        dz = (k + SIDE - dx) % SIDE
        if isinstance(i, int):
            return x_part[sign * dx % SIDE] + z_part[sign * dz % SIDE] + c_part[dc]
        return (x + sign * dx + SIDE) % SIDE * 8 + (z + sign * dz + SIDE) % SIDE * 2 + (core + dc) % 2

    def peer(q):
        jx, jz, jc = (q // 8, q // 2 % SIDE, q % 2)
        if isinstance(q, int):
            return (mate_x if jx else x) * 8 + z_part[jz] + c_part[jc]
        return (x + jx * (mate_x - x)) * 8 + (z + jz) % SIDE * 2 + (core + jc) % 2

    def seen_from(q):
        return q // 8 * 8 + (SIDE - q // 2 % SIDE) % SIDE * 2 + q % 2

    def across(i):
        return (own if i % 2 == 0 else mirror, (dp + i // 2) % DP)

    def remote(source, target, send, recv, device):
        return pltpu.make_async_remote_copy(src_ref=source, dst_ref=target, send_sem=send, recv_sem=recv, device_id=device, device_id_type=MESH_ID)
    barrier = pltpu.get_barrier_semaphore()

    @each(1, OWNERS)
    def _(i):
        pl.semaphore_signal(barrier, inc=1, device_id=at(partner(i, 1)), device_id_type=MESH_ID)
    for i in range(2, 2 * DP):
        device, plane = across(i)
        pl.semaphore_signal(barrier, inc=1, device_id=at(device, plane), device_id_type=MESH_ID)
    for steps in (-1, 1):
        pl.semaphore_signal(barrier, inc=1, device_id=shifted(steps), device_id_type=MESH_ID)
    loads = []
    for n, (source, target) in enumerate(((hidden_hbm, hidden), (gate_hbm, gate_w), (up_hbm, up_w), (down_hbm, down_w), (vocab_hbm, own_raw))):
        copy = pltpu.make_async_copy(source, target, load_sem.at[n])
        copy.start()
        loads.append(copy)
    ids[...] = jnp.zeros_like(ids)
    ids[0:2, :] = tokens_ref[...]
    ids[2:4, :] = docs_ref[...]
    pl.semaphore_wait(barrier, OWNERS - 1 + 2 * (DP - 1) + 2)

    def columns(plane):
        return pl.ds(pl.multiple_of(plane * quarter, quarter), quarter)

    def voc_across(piece):
        span = pl.ds(pl.multiple_of(dp * quarter + piece * (quarter // 2), quarter // 2), quarter // 2)
        n = piece * DP
        return remote(vocab_hbm.at[:, span], other_raw.at[:, span], send_voc.at[n], recv_voc.at[n], at(mirror))

    def voc_along(dy, source):
        return remote(other_raw.at[:, columns(source)], other_raw.at[:, columns(source)], send_voc.at[dy], recv_voc.at[dy], at(own, (dp + dy) % DP))

    def ids_copy():
        return remote(ids, next_ids, send_ids, recv_ids, shifted(-1))
    ids_copy().start()
    for piece in range(2):
        voc_across(piece).start()
    loads[0].wait()
    normed[...] = normalize(hidden[...].astype(jnp.float32), gain_ref[...]).astype(jnp.bfloat16)
    first = routes_ref[0:1, :]
    second = routes_ref[1:2, :]
    expert_iota = lax.broadcasted_iota(jnp.int32, (experts, tokens), 0)
    is_first = expert_iota == first
    is_second = expert_iota == second
    member = jnp.where(is_first | is_second, 1.0, 0.0).astype(jnp.bfloat16)
    earlier = lax.broadcasted_iota(jnp.int32, (tokens, tokens), 0) < lax.broadcasted_iota(jnp.int32, (tokens, tokens), 1)
    rank = jnp.dot(member, jnp.where(earlier, 1.0, 0.0).astype(jnp.bfloat16), preferred_element_type=jnp.float32)

    def position(expert, chosen):
        owner = expert // local
        dx = (owner // 8 + SIDE - x) % SIDE
        dz = (owner // 2 % SIDE + SIDE - z) % SIDE
        dc = (owner + core) % 2
        k = (dx + dz) % SIDE
        index = dc * 16 + k * 4 + dx
        own_rank = jnp.sum(jnp.where(chosen, rank, 0.0), axis=0, keepdims=True).astype(jnp.int32)
        return index * part + expert % local * slots + own_rank
    first_pos = position(first, is_first)
    second_pos = position(second, is_second)

    def slot_rows(i):
        return pl.ds(i * slots if isinstance(i, int) else pl.multiple_of(i * slots, slots), slots)

    def out(i):
        return remote(outgoing.at[i], arrived.at[:, slot_rows(i)], send_out.at[i], recv_out.at[i], at(partner(i, 1)))

    def back(i):
        return remote(result.at[:, slot_rows(i)], returned.at[i], send_back.at[i], recv_back.at[i], at(partner(i, -1)))
    for group in range(GROUPS):
        slot_iota = lax.broadcasted_iota(jnp.int32, (per_group * part, tokens), 0) + group * per_group * part
        chosen = (slot_iota == first_pos) | (slot_iota == second_pos)
        block = jnp.dot(jnp.where(chosen, 1.0, 0.0).astype(jnp.bfloat16), normed[...], preferred_element_type=jnp.float32)
        outgoing[pl.ds(group * per_group, per_group)] = block.astype(jnp.bfloat16).reshape(per_group, local, slots, width)
        if group == 0:
            own_copy = pltpu.make_async_copy(outgoing.at[0], arrived.at[:, pl.ds(0, slots)], self_sem)
            own_copy.start()

        @each(max(1, group * per_group), (group + 1) * per_group)
        def _(i):
            out(i).start()
    ids_copy().wait_recv()
    row_iota = lax.broadcasted_iota(jnp.int32, ids.shape, 0)
    lane_iota = lax.broadcasted_iota(jnp.int32, ids.shape, 1)
    own_ids = ids[...]
    after = pltpu.roll(own_ids, half - 1, 1)
    ends = lane_iota == half - 1
    after = jnp.where(ends & (row_iota == 0), own_ids[1:2, 0:1], after)
    after = jnp.where(ends & (row_iota == 1), next_ids[0:1, 0:1], after)
    after = jnp.where(ends & (row_iota == 2), own_ids[3:4, 0:1], after)
    after = jnp.where(ends & (row_iota == 3), next_ids[2:3, 0:1], after)
    targets[0] = after

    def target_copy(q):
        there = seen_from(q)
        return remote(targets.at[0], targets.at[there], send_tgt.at[q], recv_tgt.at[there], at(peer(q)))

    @each(1, PEERS)
    def _(q):
        target_copy(q).start()
    router_scores = lax.dot_general(router_ref[...], normed[...], (((1,), (1,)), ((), ())), preferred_element_type=jnp.float32)
    picked = jnp.sum(jnp.where(is_first, router_scores, 0.0) - jnp.where(is_second, router_scores, 0.0), axis=0, keepdims=True)
    first_gate = jax.nn.sigmoid(picked)
    lines = lax.broadcasted_iota(jnp.int32, (128, tokens), 0)
    table = jnp.where(lines == 0, first_pos.astype(jnp.float32), jnp.where(lines == 1, second_pos.astype(jnp.float32), jnp.where(lines == 2, first_gate, 0.0)))
    per_token = table.T
    place_iota = lax.broadcasted_iota(jnp.int32, (tokens, experts * slots), 1).astype(jnp.float32)
    place_a[...] = jnp.where(place_iota == per_token[:, 0:1], 1.0, 0.0).astype(jnp.bfloat16)
    place_b[...] = jnp.where(place_iota == per_token[:, 1:2], 1.0, 0.0).astype(jnp.bfloat16)
    gate_a = per_token[:, 2:3]
    gate_b = 1.0 - gate_a
    loads[4].wait()

    @pl.loop(0, voc // 128)
    def _(j):
        strip = pl.ds(pl.multiple_of(j * 128, 128), 128)
        vocab_t[strip, :] = own_raw[:, strip].T
    voc_across(0).wait_recv()
    voc_across(1).wait_recv()
    for dy in range(1, DP):
        voc_along(dy, dp).start()
    own_copy.wait()
    for copy in loads[1:4]:
        copy.wait()
    for group in range(GROUPS):
        low, high = (max(1, group * per_group), (group + 1) * per_group)

        @each(low, high)
        def _(i):
            out(i).wait_recv()

        @pl.loop(0, local)
        def _(n):
            inputs = arrived[n, pl.ds(group * chunk, chunk)]
            gate_part = jnp.dot(inputs, gate_w[n], preferred_element_type=jnp.float32)
            up_part = jnp.dot(inputs, up_w[n], preferred_element_type=jnp.float32)
            active = (jax.nn.silu(gate_part) * up_part).astype(jnp.bfloat16)
            result[n, pl.ds(group * chunk, chunk)] = jnp.dot(active, down_w[n], preferred_element_type=jnp.float32).astype(jnp.bfloat16)
        if group == 0:
            home = pltpu.make_async_copy(result.at[:, pl.ds(0, slots)], returned.at[0], self_sem)
            home.start()

        @each(low, high)
        def _(i):
            back(i).start()
    for dy in range(DP):
        source = (dp + DP - dy) % DP
        if dy:
            voc_along(dy, source).wait_recv()

        @pl.loop(0, quarter // 128)
        def _(j):
            start = source * quarter + j * 128
            vocab_t[pl.ds(pl.multiple_of(voc + start, 128), 128), :] = other_raw[:, pl.ds(pl.multiple_of(start, 128), 128)].T
    above = x * 8 + (z + 1) % SIDE * 2 + core
    below = x * 8 + (z + SIDE - 1) % SIDE * 2 + core
    mate = mate_x * 8 + z * 2 + core
    sibling = x * 8 + z * 2 + 1 - core
    sends = []

    def row_copy(slot, h, there, device, side=0):
        number = len(sends)

        def made():
            return remote(rows.at[slot, h, 0], rows.at[there, h, side], send_rows.at[number], recv_rows.at[(there * 2 + h) * 2 + side], at(device))
        sends.append(made)
        return made

    def row_arrival(slot, h, side):
        return remote(rows.at[slot, h, side], rows.at[slot, h, side], send_rows.at[0], recv_rows.at[(slot * 2 + h) * 2 + side], at(sibling))
    copies = {}
    moves = [move for moves in (FIRST_SENDS, *(entry[1:] for entry in SCHEDULE)) for move in moves if len(move) == 3]
    for slot, h, way in moves:
        jx, jz = (slot // SIDE, slot % SIDE)
        if way == ABOVE:
            copies[slot, h, way] = row_copy(slot, h, jx * SIDE + (jz + 3) % SIDE, above)
        elif way == BELOW:
            copies[slot, h, way] = row_copy(slot, h, jx * SIDE + (jz + 1) % SIDE, below)
        elif way == MATE:
            copies[slot, h, way] = row_copy(slot, h, (1 - jx) * SIDE + jz, mate)
        else:
            copies[slot, h, way] = row_copy(slot, h, slot, sibling, 1)
    home.wait()
    for i in range(1, OWNERS):
        out(i).wait_send()
    for q in range(1, PEERS):
        target_copy(q).wait_send()
    voc_across(0).wait_send()
    voc_across(1).wait_send()
    ids_copy().wait_send()
    mixed[...] = hidden[...].astype(jnp.float32)
    for group in range(GROUPS):
        low, high = (max(1, group * per_group), (group + 1) * per_group)

        @each(low, high)
        def _(i):
            back(i).wait_recv()
        block = returned[pl.ds(group * per_group, per_group)].reshape(per_group * part, width)
        span = slice(group * per_group * part, (group + 1) * per_group * part)

        def add(lines):
            return mixed[lines, :] + (gate_a[lines] * jnp.dot(place_a[lines, span], block, preferred_element_type=jnp.float32) + gate_b[lines] * jnp.dot(place_b[lines, span], block, preferred_element_type=jnp.float32))
        if group < GROUPS - 1:
            mixed[...] = add(slice(0, tokens))
        else:
            for h in range(2):
                lines = slice(h * half, (h + 1) * half)
                rows[0, h, 0] = normalize(add(lines), final_gain_ref[...]).astype(jnp.bfloat16)
                for move in FIRST_SENDS:
                    if move[1] == h:
                        copies[move]().start()

    @each(1, PEERS)
    def _(q):
        target_copy(seen_from(q)).wait_recv()
    own_base = own * voc
    other_base = mirror * voc
    tile = voc

    def stats_copy(q):
        there = seen_from(q)
        return remote(stats_out.at[q], stats_in.at[there], send_stats.at[q], recv_stats.at[there], at(peer(q)))

    @pl.loop(0, PEERS)
    def _(q):
        stats_out[q] = jnp.zeros(stats_out.shape[1:], jnp.float32)

    @pl.loop(0, len(SCHEDULE))
    def _(step):
        slot = looked_up([entry[0][0] for entry in SCHEDULE], step)
        h = looked_up([entry[0][1] for entry in SCHEDULE], step)
        for k, entry in enumerate(SCHEDULE):
            if len(entry) == 1:
                continue

            @pl.when(step == k)
            def _():
                for move in entry[1:]:
                    if len(move) == 2:
                        row_arrival(*move, 0).wait_recv()
                    else:
                        copies[move]().start()
        row_arrival(slot, h, 1).wait_recv()
        block = rows[slot, h].reshape(2 * half, width)
        wanted = jnp.concatenate([targets[2 * slot, pl.ds(h, 1), :], targets[2 * slot + 1, pl.ds(h, 1), :]], axis=1)
        high = total = hit = None
        for n in range(2):
            scores = lax.dot_general(vocab_t[n * tile:(n + 1) * tile, :], block, (((1,), (1,)), ((), ())), preferred_element_type=jnp.float32)
            base = own_base if n == 0 else other_base
            match = lax.broadcasted_iota(jnp.int32, scores.shape, 0) == wanted - base
            stacked = scores.reshape(tile // 8, 8, 2 * half)
            found = jnp.sum(jnp.where(match, scores, 0.0).reshape(stacked.shape), axis=0)
            top = jnp.max(stacked, axis=0)
            if n:
                top = jnp.maximum(top, high)
            summed = jnp.sum(jnp.exp(stacked - top[None]), axis=0)
            if n:
                summed = summed + total * jnp.exp(high - top)
                found = found + hit
            high, total, hit = (top, summed, found)
        top = jnp.max(high, axis=0, keepdims=True)
        summed = jnp.sum(total * jnp.exp(high - top), axis=0, keepdims=True)
        found = jnp.sum(hit, axis=0, keepdims=True)
        for side in range(2):
            lanes = slice(side * half, (side + 1) * half)
            stats_out[2 * slot + side, pl.ds(h, 1), :] = top[:, lanes]
            stats_out[2 * slot + side, pl.ds(2 + h, 1), :] = summed[:, lanes]
            stats_out[2 * slot + side, pl.ds(4 + h, 1), :] = found[:, lanes]
        last = looked_up([int(all((e[0] != entry[0] and e[0][0] != entry[0][0] for e in SCHEDULE[k + 1:]))) for k, entry in enumerate(SCHEDULE)], step)

        @pl.when(last == 1)
        def _():

            @pl.when(slot > 0)
            def _():
                stats_copy(2 * slot).start()
            stats_copy(2 * slot + 1).start()
    stats_in[0] = stats_out[0]

    @each(1, PEERS)
    def _(q):
        stats_copy(seen_from(q)).wait_recv()
    every = stats_in[...]
    top = jnp.max(every[:, 0:2], axis=0)
    summed = jnp.sum(every[:, 2:4] * jnp.exp(every[:, 0:2] - top[None]), axis=0)
    found = jnp.sum(every[:, 4:6], axis=0)
    docs = docs_ref[...]
    two_rows = lax.broadcasted_iota(jnp.int32, docs.shape, 0)
    two_lanes = lax.broadcasted_iota(jnp.int32, docs.shape, 1)
    at_end = (two_rows == 1) & (two_lanes == half - 1) & (linear == devices - 1)
    counted = (targets[0, 2:4, :] == docs) & jnp.logical_not(at_end)
    token_loss = jnp.where(counted, top + jnp.log(summed) - found, 0.0)
    made_ref[0:2, :] = token_loss

    def whole(values):
        return jnp.sum(jnp.sum(values, axis=1, keepdims=True), axis=0, keepdims=True)

    def of_document(number):
        mask = docs == number
        return (whole(jnp.where(mask, token_loss, 0.0)), whole(jnp.where(mask, 1.0, 0.0)))
    lead_loss, lead_length = of_document(DOC_DEV * linear - 1)
    lines = lax.broadcasted_iota(jnp.int32, (8, 128), 0)
    sums_out[...] = jnp.where(lines == 0, whole(token_loss), jnp.where(lines == 1, lead_loss, jnp.where(lines == 2, lead_length, 0.0)))

    def sum_copy(q):
        there = seen_from(q)
        return remote(sums_out, sums_in.at[there], send_sums.at[q], recv_sums.at[there], at(peer(q)))

    def wide_copy(i):
        device, plane = across(i)
        return remote(wide_out, wide_in.at[i], send_wide.at[i], recv_wide.at[i], at(device, plane))

    def lead_copy():
        return remote(sums_out, lead_in, send_lead, recv_lead, shifted(-1))
    for q in range(1, PEERS):
        sum_copy(q).start()
    lead_copy().start()
    sums_in[0] = sums_out[...]
    parts = [of_document(DOC_DEV * linear + j) for j in range(DOC_DEV)]
    for i in range(1, OWNERS):
        back(i).wait_send()
    for dy in range(1, DP):
        voc_along(dy, dp).wait_send()
    for q in range(1, PEERS):
        sum_copy(seen_from(q)).wait_recv()
    wide_out[...] = jnp.sum(sums_in[...], axis=0)
    for i in range(1, 2 * DP):
        wide_copy(i).start()
    wide_in[0] = wide_out[...]
    for made in sends:
        made().wait_send()
    for q in range(1, PEERS):
        stats_copy(q).wait_send()
    lead_copy().wait_recv()
    for i in range(1, 2 * DP):
        wide_copy(i).wait_recv()
    global_sum = jnp.sum(wide_in[...], axis=0)[0:1, 0:1]
    global_mean = global_sum / (tokens * devices - DOC_DEV * devices)
    lanes = lax.broadcasted_iota(jnp.int32, (1, 128), 1)
    scores = jnp.zeros((1, 128), jnp.float32)
    for j, (part_loss, part_length) in enumerate(parts):
        if j == DOC_DEV - 1:
            part_loss = part_loss + lead_in[1:2, 0:1]
            part_length = part_length + lead_in[2:3, 0:1]
        scores = jnp.where(lanes == j, part_loss / part_length - global_mean, scores)
    made_ref[2:3, :] = scores
    for q in range(1, PEERS):
        sum_copy(q).wait_send()
    for i in range(1, 2 * DP):
        wide_copy(i).wait_send()
    lead_copy().wait_send()


def local(hidden_in, moe_gain, router_weight, expert_gate, expert_up, expert_down, final_gain, vocab_weight, token_ids, doc_ids, routes):
    tokens, width = hidden_in.shape
    here, _, hidden_units = expert_gate.shape
    voc = vocab_weight.shape[1]
    experts = OWNERS * here
    slots = max(2, 2 * TOP * tokens // experts)
    half = tokens // 2
    bf16, f32, i32 = (jnp.bfloat16, jnp.float32, jnp.int32)
    vmem = pl.BlockSpec(memory_space=pltpu.VMEM)
    hbm = pl.BlockSpec(memory_space=pl.ANY)
    dma = pltpu.SemaphoreType.DMA
    made = pl.pallas_call(kernel, out_shape=jax.ShapeDtypeStruct((8, half), f32), in_specs=[hbm] + [vmem] * 6 + [hbm] * 4, out_specs=vmem, scratch_shapes=[pltpu.VMEM((tokens, width), bf16), pltpu.VMEM((tokens, width), bf16), pltpu.VMEM((OWNERS, here, slots, width), bf16), pltpu.VMEM((here, OWNERS * slots, width), bf16), pltpu.VMEM((here, width, hidden_units), bf16), pltpu.VMEM((here, width, hidden_units), bf16), pltpu.VMEM((here, hidden_units, width), bf16), pltpu.VMEM((here, OWNERS * slots, width), bf16), pltpu.VMEM((OWNERS, here, slots, width), bf16), pltpu.VMEM((tokens, experts * slots), bf16), pltpu.VMEM((tokens, experts * slots), bf16), pltpu.VMEM((tokens, width), f32), pltpu.VMEM((width, voc), bf16), pltpu.VMEM((width, voc), bf16), pltpu.VMEM((2 * voc, width), bf16), pltpu.VMEM((8, 2, 2, half, width), bf16), pltpu.VMEM((8, half), i32), pltpu.VMEM((8, half), i32), pltpu.VMEM((PEERS, 8, half), i32), pltpu.VMEM((PEERS, 8, half), f32), pltpu.VMEM((PEERS, 8, half), f32), pltpu.VMEM((8, 128), f32), pltpu.VMEM((PEERS, 8, 128), f32), pltpu.VMEM((8, 128), f32), pltpu.VMEM((8, 128), f32), pltpu.VMEM((2 * DP, 8, 128), f32), dma((5,)), dma, dma((OWNERS,)), dma((OWNERS,)), dma((OWNERS,)), dma((OWNERS,)), dma((DP + 1,)), dma((DP + 1,)), dma, dma, dma((PEERS,)), dma((PEERS,)), dma((32,)), dma((32,)), dma((PEERS,)), dma((PEERS,)), dma((PEERS,)), dma((PEERS,)), dma, dma, dma((2 * DP,)), dma((2 * DP,))], compiler_params=pltpu.CompilerParams(collective_id=0, has_side_effects=True, vmem_limit_bytes=58 * 2 ** 20), name='scoring')(hidden_in, moe_gain.reshape(1, width), router_weight.T, routes.T, final_gain.reshape(1, width), token_ids.reshape(2, half), doc_ids.reshape(2, half), expert_gate, expert_up, expert_down, vocab_weight)
    return (made[0:2].reshape(tokens), made[2, :DOC_DEV])

def solution(mesh):
    in_specs = (P(BOTH, None), P(), P(), P('expert', None, None), P('expert', None, None), P('expert', None, None), P(), P(None, 'expert'), P(BOTH), P(BOTH), P(BOTH, None))
    return jax.shard_map(local, mesh=mesh, in_specs=in_specs, out_specs=(P(BOTH), P(BOTH)), check_vma=False)
```
